32 devices in a mesh: fsdp: 8 (over y, x, core), tp: 4 (over z).
Axes of the slice: x: 2, y: 2, z: 4, core: 2. Of those that a mesh axis runs over, the one named last changes fastest.
Arguments:
- grads: bfloat16 [64, 128, 8192], P('tp', None, 'fsdp'), may hold values from -60 to 60
- momentum: bfloat16 [64, 128, 8192], P('tp', None, 'fsdp'), may hold values from -6 to 6
- owner_table: int32 [64, 1], P('tp'), may hold values from 0 to 7; in each aligned block of 16 rows (0 to 15, 16 to 31, ...) at most 2 rows name the same one
- pool_map: int32 [4, 16], P('tp'), may hold values from 0 to 15, each once within a row
Outputs:
- new_momentum: bfloat16 [64, 128, 8192], P('tp', None, 'fsdp')
- pool_update: bfloat16 [64, 128, 8192], P('tp', None, 'fsdp')
- slot_rms: float32 [4, 16], P('tp', 'fsdp')
The draws below stay inside these ranges and needn't reach their ends.
Inputs may be any that keep to these rules, and one draw needn't show every extreme that they name: `owner_table`: within each aligned block of 16 rows (the head blocks of one index of tp) no owner is named more than 2 times. `pool_map`: each row is a permutation of 0 to 15.
All inputs are finite; a program needn't handle non-finite values.
Results may differ from the reference program's by a relative error of at most 0.0058.
Values may be sent and summed in bfloat16 or wider, within the bound.
No kernel may reach another device: no remote copies, remote signals or barrier semaphores. Data moves between devices by JAX's collectives and lax.ppermute only.
A program may use at most 64 MiB of HBM per device.

```python
import math
import jax
import jax.numpy as jnp
import numpy as np
from jax import lax

D = 8192
HEAD = 128
NB_ROW = 16
CAP = 2
ITERS = 3
NBLK = 64
N_FSDP = 8
N_TP = 4


def draw_grads(key, part):
    keys = jax.random.split(jax.random.fold_in(key, 17), 3)
    row_scale = jnp.exp(jax.random.uniform(keys[0], (NBLK, HEAD, 1), jnp.float32, math.log(0.3), math.log(3.0)))
    col_scale = jnp.exp(jax.random.uniform(keys[1], (NBLK, 1, D), jnp.float32, math.log(0.3), math.log(3.0)))
    values = jnp.clip(jax.random.normal(keys[2], (NBLK, HEAD, D), jnp.float32), -6.0, 6.0)
    return (values * row_scale * col_scale).astype(jnp.bfloat16)


def shard_levels(rng, shape, shards, least, high):
    def one(dim, parts):
        draws = jax.random.uniform(jax.random.fold_in(jax.random.fold_in(rng, 6), dim), (parts,), jnp.float32, least / len(shards), high / len(shards))
        return jnp.repeat(jnp.exp(draws), shape[dim] // parts).reshape((-1,) + (1,) * (len(shape) - dim - 1))

    level = one(*shards[0])
    for cut in shards[1:]:
        level = level * one(*cut)
    return level


def shared_out(stream_key, own, number, rows, number_of, top, limit, slope):
    ranking = jax.random.permutation(stream_key, number_of)
    heavy_load, usual = shares(number_of, rows * top, limit, slope, True), shares(number_of, rows * top, limit, slope, False)
    places = jnp.arange(number_of)

    def named(tallies, offset_by):
        used = int((tallies > 0).sum())
        fixed = max(1, used // 4)
        moved = fixed + (places - fixed + offset_by * (used - fixed)) % max(1, number_of - fixed)
        return jnp.zeros((number_of,), jnp.int32).at[ranking[jnp.where(places < fixed, places, moved)]].set(jnp.asarray(tallies, jnp.int32))

    tallies = jnp.where(number % 4 == 0, named(heavy_load, number // 4), named(usual, number - number // 4 - 1))
    mixed = jax.random.permutation(jax.random.fold_in(own, 3), number_of)
    source_of, taker = mixed[0:number_of // 2 * 2:2], mixed[1:number_of // 2 * 2:2]
    margin = jnp.minimum(tallies[source_of] - 1, limit - tallies[taker]) // 2
    margin = jnp.where((source_of == ranking[0]) | (taker == ranking[0]) | (tallies[taker] == 0), 0, jnp.maximum(margin, 0))
    moved = jax.random.randint(jax.random.fold_in(own, 4), (number_of // 2,), 0, 1 << 20) % (margin + 1)
    tallies = tallies.at[source_of].add(-moved).at[taker].add(moved)
    members = jnp.searchsorted(jnp.cumsum(tallies), jnp.arange(rows * top), side="right").astype(jnp.int32)
    grid = members.reshape(top, rows).T
    grid = grid[jax.random.permutation(jax.random.fold_in(own, 1), rows)]
    offset_by = jax.random.randint(jax.random.fold_in(own, 2), (rows, 1), 0, top)
    return jnp.take_along_axis(grid, (jnp.arange(top)[None, :] + offset_by) % top, axis=1)


def shares(number_of, total, limit, slope, full):
    loads = [(1 << 20) // math.isqrt(rank ** slope) + 1 for rank in range(1, number_of + 1)]
    largest = limit if full else min(limit, max(-(-total // number_of), total * loads[0] // sum(loads)))
    least = 1 if total - largest >= number_of - 1 else 0
    holding, rest = [largest] + [least] * (number_of - 1), total - largest - least * (number_of - 1)
    while rest > 0:
        candidates = [i for i in range(1, number_of) if holding[i] < largest] or [i for i in range(1, number_of) if holding[i] < limit]
        whole, budget = sum([loads[i] for i in candidates]), rest
        for i in candidates:
            more = min(limit - holding[i], max(1, budget * loads[i] // whole), rest)
            holding[i] = holding[i] + more
            rest = rest - more
    return np.array(holding)


def normal_values(rng, extent, spread, most, pieces=(), held_as=jnp.bfloat16):
    array = spread * jax.random.normal(rng, extent, jnp.float32)
    if pieces:
        array = array * shard_levels(rng, extent, pieces, -0.22, 0.18)
    return jnp.clip(array, -most, most).astype(held_as)


def setup_inputs(seed: int = 0) -> dict:
    key_of = jax.random.split(jax.random.key(seed), 5)
    grads = draw_grads(jax.random.fold_in(key_of[4], 71), 0)
    momentum = normal_values(key_of[1], (NBLK, HEAD, D), 1.0, 6.0, ((0, 4), (2, 8)))
    owner_table_keys = jax.random.split(jax.random.fold_in(key_of[2], 1), NBLK // NB_ROW)
    owner_table_turns = jax.random.permutation(jax.random.fold_in(key_of[2], 3), NBLK // NB_ROW)
    owner_table = jax.vmap(lambda own, number: shared_out(jax.random.fold_in(key_of[2], 2), own, number, NB_ROW, N_FSDP, 1, CAP, 2))(owner_table_keys, owner_table_turns).reshape((NBLK, 1))
    pool_map = jax.vmap(lambda own: jax.random.permutation(own, NB_ROW))(jax.random.split(key_of[3], N_TP)).reshape((N_TP, NB_ROW)).astype(jnp.int32)
    return dict(grads=grads, momentum=momentum, owner_table=owner_table, pool_map=pool_map)


momentum_rate = 0.95
step_size = 0.8
epsilon = 1e-07
poly_linear = 3.4445
poly_cubic = -4.775
poly_quintic = 2.0315

def newton_schulz(block):
    values = block.astype(jnp.float32)
    squares = jnp.sum(values * values)
    inverse = 1.0 / (jnp.sqrt(squares) + epsilon)
    gram = jnp.dot(values, values.T, precision=lax.Precision.HIGHEST) * (inverse * inverse)
    identity = jnp.eye(gram.shape[0], dtype=jnp.float32)
    transform = identity
    for _ in range(ITERS):
        square_gram = jnp.dot(gram, gram, precision=lax.Precision.HIGHEST)
        mixed = poly_linear * identity + poly_cubic * gram + poly_quintic * square_gram
        transform = jnp.dot(mixed, transform, precision=lax.Precision.HIGHEST)
        gram = jnp.dot(mixed, jnp.dot(gram, mixed, precision=lax.Precision.HIGHEST), precision=lax.Precision.HIGHEST)
    current = jnp.dot(transform * inverse, values, precision=lax.Precision.HIGHEST)
    return (current.astype(jnp.bfloat16), squares)

def reference(grads, momentum, owner_table, pool_map):
    velocity = momentum_rate * momentum.astype(jnp.float32) + grads.astype(jnp.float32)
    new_momentum = velocity.astype(jnp.bfloat16)
    nesterov = (grads.astype(jnp.float32) + momentum_rate * velocity).astype(jnp.bfloat16)
    ortho, squares = lax.map(newton_schulz, nesterov)
    factor = step_size * 0.2 * math.sqrt(D)
    update = (-factor * ortho.astype(jnp.float32)).astype(jnp.bfloat16)
    group = NB_ROW // N_TP
    row_index = jnp.arange(NBLK, dtype=jnp.int32) // NB_ROW
    codes = pool_map.reshape(-1).astype(jnp.int32)
    target = codes // group * NB_ROW + row_index * group + codes % group
    pool_update = jnp.zeros_like(update).at[target].set(update)
    owners = owner_table.reshape(N_TP, NB_ROW).astype(jnp.int32)
    position = jnp.arange(NB_ROW, dtype=jnp.int32)
    earlier = position[None, :] < position[:, None]
    same_owner = owners[:, :, None] == owners[:, None, :]
    slots = lax.optimization_barrier(jnp.sum(jnp.logical_and(same_owner, earlier[None]), axis=-1)).astype(jnp.int32)
    place = row_index * (N_FSDP * CAP) + owners.reshape(-1) * CAP + slots.reshape(-1)
    rms_values = jnp.sqrt(squares / (HEAD * D))
    slot_rms = jnp.zeros((N_TP * N_FSDP * CAP,), jnp.float32).at[place].set(rms_values)
    return (new_momentum, pool_update, slot_rms.reshape(N_TP, N_FSDP * CAP))
```

```python
import functools
import math

import jax
import jax.numpy as jnp
from jax import lax
from jax.experimental import pallas as pl
from jax.experimental.pallas import tpu as pltpu
from jax.sharding import PartitionSpec as P

CAP = 2
ITERS = 3

momentum_rate = 0.95
step_size = 0.8
epsilon = 1e-07
poly_linear = 3.4445
poly_cubic = -4.775
poly_quintic = 2.0315


def nesterov_of(grads, momentum):
    g = grads.astype(jnp.float32)
    velocity = momentum_rate * momentum.astype(jnp.float32) + g
    return velocity, (g + momentum_rate * velocity).astype(jnp.bfloat16)


def first_kernel(source, g_ref, m_ref, *outs):
    step = pl.program_id(0)
    _, y = nesterov_of(g_ref[0], m_ref[0])
    for i, out in enumerate(outs):

        @pl.when(step == i)
        def _():
            out[0] = y


def first_blocks(source, grads, momentum, count):
    block = (1,) + grads.shape[1:]
    return pl.pallas_call(
        first_kernel,
        out_shape=[jax.ShapeDtypeStruct(block, jnp.bfloat16)] * count,
        grid_spec=pltpu.PrefetchScalarGridSpec(
            num_scalar_prefetch=1,
            grid=(count,),
            in_specs=[pl.BlockSpec(block, lambda i, source: (source[i], 0, 0))] * 2,
            out_specs=[pl.BlockSpec(block, lambda i, source: (0, 0, 0))] * count,
        ),
        name="first_blocks",
    )(source, grads, momentum)


def all_kernel(starts, source, place, g_ref, m_ref, newm_ref, gram_ref, diag_ref, *outs):
    step = pl.program_id(0)
    velocity, y = nesterov_of(g_ref[0], m_ref[0])
    newm_ref[0] = velocity.astype(jnp.bfloat16)
    gram = lax.dot_general(y, y, (((1,), (1,)), ((), ())), preferred_element_type=jnp.float32)
    gram_ref[0] = gram
    rows = lax.broadcasted_iota(jnp.int32, gram.shape, 0)
    columns = lax.broadcasted_iota(jnp.int32, gram.shape, 1)
    diagonal = jnp.sum(jnp.where(rows == columns, gram, 0.0), axis=0, keepdims=True)
    diag_ref[pl.ds(place[step], 1), :] = diagonal
    for (start, count), out in zip(starts, outs):

        @pl.when(jnp.logical_and(step >= start, step < start + count))
        def _():
            out[0] = y


def all_blocks(source, place, grads, momentum, starts):
    blocks, head, width = grads.shape
    block = (1, head, width)

    def chunk_spec(start, count):
        return pl.BlockSpec(block, lambda i, s, p: (jnp.clip(i - start, 0, count - 1), 0, 0))

    return pl.pallas_call(
        functools.partial(all_kernel, starts),
        out_shape=[
            jax.ShapeDtypeStruct(grads.shape, jnp.bfloat16),
            jax.ShapeDtypeStruct((blocks, head, head), jnp.float32),
            jax.ShapeDtypeStruct((blocks, head), jnp.float32),
        ]
        + [jax.ShapeDtypeStruct((count, head, width), jnp.bfloat16) for _, count in starts],
        grid_spec=pltpu.PrefetchScalarGridSpec(
            num_scalar_prefetch=2,
            grid=(blocks,),
            in_specs=[pl.BlockSpec(block, lambda i, s, p: (s[i], 0, 0))] * 2,
            out_specs=[
                pl.BlockSpec(block, lambda i, s, p: (s[i], 0, 0)),
                pl.BlockSpec((1, head, head), lambda i, s, p: (p[i], 0, 0)),
                pl.BlockSpec((blocks, head), lambda i, s, p: (0, 0)),
            ]
            + [chunk_spec(start, count) for start, count in starts],
        ),
        name="all_blocks",
    )(source, place, grads, momentum)


def apply_kernel(factor, starts, place, q_ref, *refs):
    step = pl.program_id(0)
    out = refs[-1]
    q = q_ref[0]
    high = q.astype(jnp.bfloat16)
    low = (q - high.astype(jnp.float32)).astype(jnp.bfloat16)
    for (start, count), y_ref in zip(starts, refs):

        @pl.when(jnp.logical_and(step >= start, step < start + count))
        def _():
            y = y_ref[0]
            ortho = jnp.dot(high, y, preferred_element_type=jnp.float32)
            ortho = ortho + jnp.dot(low, y, preferred_element_type=jnp.float32)
            ortho = ortho.astype(jnp.bfloat16).astype(jnp.float32)
            out[0] = (-factor * ortho).astype(jnp.bfloat16)


def apply_blocks(factor, place, transforms, chunks, into):
    head, width = chunks[0].shape[1:]
    blocks = transforms.shape[0]
    block = (1, head, width)
    starts, total = [], 0
    for chunk in chunks:
        starts.append((total, chunk.shape[0]))
        total += chunk.shape[0]

    def chunk_spec(start, count):
        return pl.BlockSpec(block, lambda i, p: (jnp.clip(i - start, 0, count - 1), 0, 0))

    in_specs = [pl.BlockSpec((1, head, head), lambda i, p: (p[i], 0, 0))]
    in_specs += [chunk_spec(start, count) for start, count in starts]
    operands = [transforms, *chunks]
    aliases = {}
    if into is not None:
        in_specs.append(pl.BlockSpec(memory_space=pl.ANY))
        operands.append(into)
        aliases = {len(operands): 0}
    return pl.pallas_call(
        functools.partial(apply_kernel, factor, starts),
        out_shape=jax.ShapeDtypeStruct((blocks, head, width), jnp.bfloat16),
        grid_spec=pltpu.PrefetchScalarGridSpec(
            num_scalar_prefetch=1,
            grid=(total,),
            in_specs=in_specs,
            out_specs=pl.BlockSpec(block, lambda i, p: (p[i], 0, 0)),
        ),
        input_output_aliases=aliases,
        name="apply_blocks",
    )(place, *operands)


def transforms_of(gram):
    high = lax.Precision.HIGHEST
    identity = jnp.eye(gram.shape[1], dtype=jnp.float32)[None]
    squares = jnp.sum(gram * identity, axis=(1, 2))
    inverse = 1.0 / (jnp.sqrt(squares) + epsilon)
    gram = gram * (inverse * inverse)[:, None, None]
    transform = None
    for i in range(ITERS):
        square_gram = jnp.einsum("kil,klm->kim", gram, gram, precision=high)
        mixed = poly_linear * identity + poly_cubic * gram + poly_quintic * square_gram
        if transform is None:
            transform = mixed
        else:
            transform = jnp.einsum("kil,klm->kim", mixed, transform, precision=high)
        if i + 1 < ITERS:
            right_side = jnp.einsum("kil,klm->kim", gram, mixed, precision=high)
            gram = jnp.einsum("kil,klm->kim", mixed, right_side, precision=high)
    return transform * inverse[:, None, None]


def local(grads, momentum, owner_table, pool_map):
    n_fsdp, n_tp = lax.axis_size("fsdp"), lax.axis_size("tp")
    here, row = lax.axis_index("fsdp"), lax.axis_index("tp")
    blocks, head, width = grads.shape
    group = blocks // n_tp
    paired = n_tp & (n_tp - 1) == 0

    def partner(t, x):
        return t ^ x if paired else (t + x) % n_tp

    def sender(t, x):
        return t ^ x if paired else (t - x) % n_tp

    far = [x for x in range(1, n_tp) if x >= n_tp // 2]
    near = [x for x in range(1, n_tp) if x < n_tp // 2]
    cut = max(1, group // 2)
    first = [(x, (0,)) for x in far]
    second = [(x, (c,)) for c in range(1, cut) for x in far] + [(x, tuple(range(group))) for x in near]
    late = [(x, (c,)) for c in range(cut, group) for x in far]
    own = [(0, tuple(range(group)))]
    chunks = first + second + late + own
    steps = [(x, c) for x, cs in chunks for c in cs]

    codes = pool_map[0]
    position = jnp.arange(blocks, dtype=jnp.int32)
    offsets = jnp.array([c for _, c in steps], jnp.int32)
    partners = jnp.array([x for x, _ in steps], jnp.int32)
    place_out = partner(row, partners) * group + offsets
    place_in = sender(row, partners) * group + offsets
    source = jnp.sum(jnp.where(codes[None, :] == place_out[:, None], position[None, :], 0), axis=1)

    def send(array, x):
        return lax.ppermute(array, "tp", [(t, partner(t, x)) for t in range(n_tp)])

    starts, total = [], 0
    for _, cs in chunks:
        starts.append((total, len(cs)))
        total += len(cs)

    ready = first_blocks(source[: len(first)], grads, momentum, len(first))
    got = {chunk: send(array, chunk[0]) for chunk, array in zip(first, ready)}
    rest = second + late + own
    rest_starts = starts[len(first) :]
    new_momentum, gram, diagonal, *ys = all_blocks(source, place_out, grads, momentum, rest_starts)
    ys = dict(zip(rest, ys))
    for chunk in second:
        got[chunk] = send(ys[chunk], chunk[0])

    spread = -(-blocks // n_fsdp)
    users = blocks // spread
    parts = gram.reshape(users, spread * head, head)
    parts = jnp.pad(parts, ((0, n_fsdp - users), (0, 0), (0, 0)))
    parts = jnp.concatenate([parts, jnp.broadcast_to(diagonal[None], (n_fsdp, blocks, head))], axis=1)
    arrived = lax.all_to_all(parts, "fsdp", split_axis=0, concat_axis=0, tiled=True)
    summed = jnp.sum(arrived, axis=0)
    squares = jnp.sum(summed[spread * head :], axis=1)
    transform = transforms_of(summed[: spread * head].reshape(spread, head, head))

    pairs = []
    per_row = group // spread
    for f in range(users):
        for t in range(n_tp):
            to = (t * per_row + f % per_row) * n_tp + f // per_row
            pairs.append((f * n_tp + t, to))
    transform = lax.ppermute(transform, ("fsdp", "tp"), pairs)
    transform, held = lax.optimization_barrier((transform, [ys[chunk] for chunk in late]))
    for chunk, array in zip(late, held):
        got[chunk] = send(array, chunk[0])
    spread_out = jnp.broadcast_to(transform[None], (n_fsdp,) + transform.shape)
    transforms = lax.all_to_all(spread_out, "fsdp", split_axis=0, concat_axis=0, tiled=True)
    transforms = transforms.reshape(n_fsdp * spread, head, head)[:blocks]

    owners = owner_table[:, 0]
    earlier = position[None, :] < position[:, None]
    slots = jnp.sum(jnp.logical_and(owners[:, None] == owners[None, :], earlier), axis=1)
    rms_by_place = jnp.sqrt(squares / (head * width * n_fsdp))
    by_block = jnp.sum(jnp.where(codes[:, None] == position[None, :], rms_by_place[None, :], 0.0), axis=1)
    slot_range = jnp.arange(CAP, dtype=jnp.int32)
    pick = jnp.logical_and((owners == here)[None, :], slots[None, :] == slot_range[:, None])
    slot_out = jnp.sum(jnp.where(pick, by_block[None, :], 0.0), axis=1)[None, :]

    factor = step_size * 0.2 * math.sqrt(width * n_fsdp)
    got[own[0]] = ys[own[0]]
    place_of = {}
    for chunk, (start, count) in zip(chunks, starts):
        place_of[chunk] = place_in[start : start + count]
    rounds = [own + second + first] + [[(x, (c,)) for x in far] for c in range(cut, group)]
    update = None
    for members in rounds:
        where = jnp.concatenate([place_of[chunk] for chunk in members])
        update = apply_blocks(factor, where, transforms, [got[chunk] for chunk in members], update)
    return (new_momentum, update, slot_out)


def solution(mesh):
    in_specs = (P("tp", None, "fsdp"), P("tp", None, "fsdp"), P("tp", None), P("tp", None))
    out_specs = (P("tp", None, "fsdp"), P("tp", None, "fsdp"), P("tp", "fsdp"))
    return jax.shard_map(local, mesh=mesh, in_specs=in_specs, out_specs=out_specs, check_vma=False)
```

```python
import functools
import math

import jax
import jax.numpy as jnp
from jax import lax
from jax.experimental import pallas as pl
from jax.experimental.pallas import tpu as pltpu
from jax.sharding import PartitionSpec as P


CAP = 2
ITERS = 3

momentum_rate = 0.95
step_size = 0.8
epsilon = 1e-07
poly_linear = 3.4445
poly_cubic = -4.775
poly_quintic = 2.0315


def nesterov_of(grads, momentum):
    g = grads.astype(jnp.float32)
    velocity = momentum_rate * momentum.astype(jnp.float32) + g
    return velocity, (g + momentum_rate * velocity).astype(jnp.bfloat16)


def first_kernel(wanted, pieces, codes_ref, g_ref, m_ref, *refs):
    count = len(wanted)
    outs = refs[:count]
    g_buf, m_buf, y_buf, g_sem, m_sem, y_sem = refs[count:]
    rows = g_buf.shape[2]
    group = codes_ref.shape[1] // lax.axis_size("tp")
    row = lax.axis_index("tp")

    def in_copies(i, p, source):
        part = pl.ds(p * rows, rows)
        return (
            pltpu.make_async_copy(g_ref.at[source, part], g_buf.at[i, p], g_sem.at[i, p]),
            pltpu.make_async_copy(m_ref.at[source, part], m_buf.at[i, p], m_sem.at[i, p]),
        )

    def out_copy(i, p):
        return pltpu.make_async_copy(y_buf.at[i, p], outs[i].at[0, pl.ds(p * rows, rows)], y_sem.at[i, p])

    reads = []
    for i, (place_of, c) in enumerate(wanted):
        place = place_of(row) * group + c
        source = jnp.int32(0)
        for j in range(codes_ref.shape[1]):
            source = jnp.where(codes_ref[0, j] == place, j, source)
        for p in range(pieces):
            reads.append((i, p, in_copies(i, p, source)))
            for copy in reads[-1][2]:
                copy.start()
    for i, p, copies in reads:
        for copy in copies:
            copy.wait()
        _, y = nesterov_of(g_buf[i, p], m_buf[i, p])
        y_buf[i, p] = y
        out_copy(i, p).start()
    for i, p, _ in reads:
        out_copy(i, p).wait()


def first_blocks(codes, grads, momentum, wanted, pieces=4):
    _, head, width = grads.shape
    count = len(wanted)
    buffer = pltpu.VMEM((count, pieces, head // pieces, width), jnp.bfloat16)
    return pl.pallas_call(
        functools.partial(first_kernel, wanted, pieces),
        out_shape=[jax.ShapeDtypeStruct((1, head, width), jnp.bfloat16)] * count,
        in_specs=[
            pl.BlockSpec(memory_space=pltpu.SMEM),
            pl.BlockSpec(memory_space=pl.ANY),
            pl.BlockSpec(memory_space=pl.ANY),
        ],
        out_specs=[pl.BlockSpec(memory_space=pl.ANY)] * count,
        scratch_shapes=[buffer] * 3 + [pltpu.SemaphoreType.DMA((count, pieces))] * 3,
        name="first_blocks",
    )(codes, grads, momentum)


def all_kernel(starts, source, place, g_ref, m_ref, newm_ref, gram_ref, diag_ref, *outs):
    step = pl.program_id(0)
    velocity, y = nesterov_of(g_ref[0], m_ref[0])
    newm_ref[0] = velocity.astype(jnp.bfloat16)
    gram = lax.dot_general(y, y, (((1,), (1,)), ((), ())), preferred_element_type=jnp.float32)
    gram_ref[0] = gram
    rows = lax.broadcasted_iota(jnp.int32, gram.shape, 0)
    columns = lax.broadcasted_iota(jnp.int32, gram.shape, 1)
    diagonal = jnp.sum(jnp.where(rows == columns, gram, 0.0), axis=0, keepdims=True)
    diag_ref[pl.ds(place[step], 1), :] = diagonal
    for (start, count), out in zip(starts, outs):

        @pl.when(jnp.logical_and(step >= start, step < start + count))
        def _():
            out[0] = y


def all_blocks(source, place, grads, momentum, starts):
    blocks, head, width = grads.shape
    block = (1, head, width)

    def chunk_spec(start, count):
        return pl.BlockSpec(block, lambda i, s, p: (jnp.clip(i - start, 0, count - 1), 0, 0))

    return pl.pallas_call(
        functools.partial(all_kernel, starts),
        out_shape=[
            jax.ShapeDtypeStruct(grads.shape, jnp.bfloat16),
            jax.ShapeDtypeStruct((blocks, head, head), jnp.float32),
            jax.ShapeDtypeStruct((blocks, head), jnp.float32),
        ]
        + [jax.ShapeDtypeStruct((count, head, width), jnp.bfloat16) for _, count in starts],
        grid_spec=pltpu.PrefetchScalarGridSpec(
            num_scalar_prefetch=2,
            grid=(blocks,),
            in_specs=[pl.BlockSpec(block, lambda i, s, p: (s[i], 0, 0))] * 2,
            out_specs=[
                pl.BlockSpec(block, lambda i, s, p: (s[i], 0, 0)),
                pl.BlockSpec((1, head, head), lambda i, s, p: (p[i], 0, 0)),
                pl.BlockSpec((blocks, head), lambda i, s, p: (0, 0)),
            ]
            + [chunk_spec(start, count) for start, count in starts],
        ),
        name="all_blocks",
    )(source, place, grads, momentum)


def apply_kernel(factor, starts, place, q_ref, *refs):
    step = pl.program_id(0)
    out = refs[-1]
    q = q_ref[0]
    head = q.shape[0]
    high = q.astype(jnp.bfloat16)
    low = (q - high.astype(jnp.float32)).astype(jnp.bfloat16)
    both = jnp.concatenate([high, low], axis=0)
    for (start, count), y_ref in zip(starts, refs):

        @pl.when(jnp.logical_and(step >= start, step < start + count))
        def _():
            ortho = jnp.dot(both, y_ref[0], preferred_element_type=jnp.float32)
            ortho = ortho[:head] + ortho[head:]
            ortho = ortho.astype(jnp.bfloat16).astype(jnp.float32)
            out[0] = (-factor * ortho).astype(jnp.bfloat16)


def apply_blocks(factor, place, transforms, chunks, into, tiles):
    head, width = chunks[0].shape[1:]
    blocks = transforms.shape[0]
    block = (1, head, width // tiles)
    starts, total = [], 0
    for chunk in chunks:
        starts.append((total, chunk.shape[0]))
        total += chunk.shape[0]

    def chunk_spec(start, count):
        def index(i, j, p):
            column = jnp.where(i < start, 0, jnp.where(i < start + count, j, tiles - 1))
            return (jnp.clip(i - start, 0, count - 1), 0, column)

        return pl.BlockSpec(block, index)

    in_specs = [pl.BlockSpec((1, head, head), lambda i, j, p: (p[i], 0, 0))]
    in_specs += [chunk_spec(start, count) for start, count in starts]
    operands = [transforms, *chunks]
    aliases = {}
    if into is not None:
        in_specs.append(pl.BlockSpec(memory_space=pl.ANY))
        operands.append(into)
        aliases = {len(operands): 0}
    return pl.pallas_call(
        functools.partial(apply_kernel, factor, starts),
        out_shape=jax.ShapeDtypeStruct((blocks, head, width), jnp.bfloat16),
        grid_spec=pltpu.PrefetchScalarGridSpec(
            num_scalar_prefetch=1,
            grid=(total, tiles),
            in_specs=in_specs,
            out_specs=pl.BlockSpec(block, lambda i, j, p: (p[i], 0, j)),
        ),
        input_output_aliases=aliases,
        name="apply_blocks",
    )(place, *operands)


def transforms_of(gram):
    high = lax.Precision.HIGHEST
    identity = jnp.eye(gram.shape[1], dtype=jnp.float32)[None]
    squares = jnp.sum(gram * identity, axis=(1, 2))
    inverse = 1.0 / (jnp.sqrt(squares) + epsilon)
    gram = gram * (inverse * inverse)[:, None, None]
    transform = None
    for i in range(ITERS):
        square_gram = jnp.einsum("kil,klm->kim", gram, gram, precision=high)
        mixed = poly_linear * identity + poly_cubic * gram + poly_quintic * square_gram
        if transform is None:
            transform = mixed
        else:
            transform = jnp.einsum("kil,klm->kim", mixed, transform, precision=high)
        if i + 1 < ITERS:
            right_side = jnp.einsum("kil,klm->kim", gram, mixed, precision=high)
            gram = jnp.einsum("kil,klm->kim", mixed, right_side, precision=high)
    return transform * inverse[:, None, None]


def local(grads, momentum, owner_table, pool_map):
    n_fsdp, n_tp = lax.axis_size("fsdp"), lax.axis_size("tp")
    here, row = lax.axis_index("fsdp"), lax.axis_index("tp")
    blocks, head, width = grads.shape
    group = blocks // n_tp
    paired = n_tp & (n_tp - 1) == 0

    def partner(t, x):
        return t ^ x if paired else (t + x) % n_tp

    def sender(t, x):
        return t ^ x if paired else (t - x) % n_tp

    far = [x for x in range(1, n_tp) if x >= n_tp // 2]
    near = [x for x in range(1, n_tp) if x < n_tp // 2]
    cut = max(1, group // 2)
    first = [(x, (0,)) for x in far]
    second = [(x, (c,)) for c in range(1, cut) for x in far]
    third = [(x, tuple(range(group))) for x in near]
    late = [(x, (c,)) for c in range(cut, group) for x in far]
    own = [(0, tuple(range(group)))]
    chunks = first + second + third + late + own
    steps = [(x, c) for x, cs in chunks for c in cs]

    codes = pool_map[0]
    position = jnp.arange(blocks, dtype=jnp.int32)
    offsets = jnp.array([c for _, c in steps], jnp.int32)
    partners = jnp.array([x for x, _ in steps], jnp.int32)
    place_out = partner(row, partners) * group + offsets
    place_in = sender(row, partners) * group + offsets
    source = jnp.sum(jnp.where(codes[None, :] == place_out[:, None], position[None, :], 0), axis=1)

    starts, total = {}, 0
    for chunk in chunks:
        starts[chunk] = (total, len(chunk[1]))
        total += len(chunk[1])

    got = {}

    def send(chunk, array):
        got[chunk] = lax.ppermute(array, "tp", [(t, partner(t, chunk[0])) for t in range(n_tp)])

    wanted = [(functools.partial(partner, x=x), cs[0]) for x, cs in first]
    for chunk, array in zip(first, first_blocks(pool_map, grads, momentum, wanted)):
        send(chunk, array)
    rest = second + third + late + own
    new_momentum, gram, diagonal, *ys = all_blocks(
        source, place_out, grads, momentum, [starts[chunk] for chunk in rest]
    )
    ys = dict(zip(rest, ys))
    for chunk in second + third + late:
        send(chunk, ys[chunk])

    spread = -(-blocks // n_fsdp)
    users = blocks // spread
    parts = gram.reshape(users, spread * head, head)
    parts = jnp.pad(parts, ((0, n_fsdp - users), (0, 0), (0, 0)))
    parts = jnp.concatenate([parts, jnp.broadcast_to(diagonal[None], (n_fsdp, blocks, head))], axis=1)
    arrived = lax.all_to_all(parts, "fsdp", split_axis=0, concat_axis=0, tiled=True)
    summed = jnp.sum(arrived, axis=0)
    squares = jnp.sum(summed[spread * head :], axis=1)
    transform = transforms_of(summed[: spread * head].reshape(spread, head, head))

    pairs = []
    per_row = group // spread
    for f in range(users):
        for t in range(n_tp):
            to = (t * per_row + f % per_row) * n_tp + f // per_row
            pairs.append((f * n_tp + t, to))
    transform = lax.ppermute(transform, ("fsdp", "tp"), pairs)
    spread_out = jnp.broadcast_to(transform[None], (n_fsdp,) + transform.shape)
    transforms = lax.all_to_all(spread_out, "fsdp", split_axis=0, concat_axis=0, tiled=True)
    transforms = transforms.reshape(n_fsdp * spread, head, head)[:blocks]

    owners = owner_table[:, 0]
    earlier = position[None, :] < position[:, None]
    slots = jnp.sum(jnp.logical_and(owners[:, None] == owners[None, :], earlier), axis=1)
    rms_by_place = jnp.sqrt(squares / (head * width * n_fsdp))
    by_block = jnp.sum(jnp.where(codes[:, None] == position[None, :], rms_by_place[None, :], 0.0), axis=1)
    slot_range = jnp.arange(CAP, dtype=jnp.int32)
    pick = jnp.logical_and((owners == here)[None, :], slots[None, :] == slot_range[:, None])
    slot_out = jnp.sum(jnp.where(pick, by_block[None, :], 0.0), axis=1)[None, :]

    factor = step_size * 0.2 * math.sqrt(width * n_fsdp)
    for chunk in own:
        got[chunk] = ys[chunk]
    rounds = [own + first + second]
    if third:
        rounds.append(third)
    rounds += [late[i : i + len(far)] for i in range(0, len(late) - len(far), len(far))]
    rounds += [[chunk] for chunk in late[-len(far) :]]
    rounds = [members for members in rounds if members]
    update = None
    for members in rounds:
        where = jnp.concatenate([place_in[s : s + n] for s, n in (starts[chunk] for chunk in members)])
        tiles = 1 if len(where) > 2 or width < 512 else 4
        update = apply_blocks(factor, where, transforms, [got[chunk] for chunk in members], update, tiles)
    return (new_momentum, update, slot_out)


def solution(mesh):
    def step(*args):
        return local(*args)

    in_specs = (P("tp", None, "fsdp"), P("tp", None, "fsdp"), P("tp", None), P("tp", None))
    out_specs = (P("tp", None, "fsdp"), P("tp", None, "fsdp"), P("tp", "fsdp"))
    step = jax.shard_map(step, mesh=mesh, in_specs=in_specs, out_specs=out_specs, check_vma=False)
    return step
```

```python
import functools
import math

import jax
import jax.numpy as jnp
from jax import lax
from jax.experimental import pallas as pl
from jax.experimental.pallas import tpu as pltpu
from jax.sharding import PartitionSpec as P


CAP = 2
ITERS = 3

momentum_rate = 0.95
step_size = 0.8
epsilon = 1e-07
poly_linear = 3.4445
poly_cubic = -4.775
poly_quintic = 2.0315


HBM = pl.BlockSpec(memory_space=pltpu.HBM)
SMEM = pl.BlockSpec(memory_space=pltpu.SMEM)
VMEM = pl.BlockSpec(memory_space=pltpu.VMEM)


def nesterov_of(grads, momentum):
    g = grads.astype(jnp.float32)
    velocity = momentum_rate * momentum.astype(jnp.float32) + g
    return velocity, (g + momentum_rate * velocity).astype(jnp.bfloat16)


def iotas(shape):
    return lax.broadcasted_iota(jnp.int32, shape, 0), lax.broadcasted_iota(jnp.int32, shape, 1)


def diagonal_of(square):
    rows, columns = iotas(square.shape)
    return jnp.sum(jnp.where(rows == columns, square, 0.0), axis=0, keepdims=True)


def pack(square):
    half = square.shape[0] // 2
    rows, columns = iotas((half, 2 * half))
    lower = jnp.concatenate([square[half:, half:], square[half:, :half]], axis=1)
    return jnp.where(columns >= rows, square[:half], lower)


def unpack(packed, diagonal):
    half = packed.shape[0]
    rows, columns = iotas(packed.shape)
    top = jnp.where(columns > rows, packed, 0.0)
    turned = jnp.concatenate([packed[:, half:], packed[:, :half]], axis=1)
    keep = jnp.logical_and(columns >= half, columns - half < rows)
    strict = jnp.concatenate([top, jnp.where(keep, turned, 0.0)], axis=0)
    rows, columns = iotas(strict.shape)
    return strict + strict.T + jnp.where(rows == columns, diagonal, 0.0)


def first_kernel(wanted, pieces, codes_ref, g_ref, m_ref, *refs):
    count = len(wanted)
    outs = refs[:count]
    g_buf, m_buf, y_buf, g_sem, m_sem, y_sem = refs[count:]
    rows = g_buf.shape[2]
    group = codes_ref.shape[1] // lax.axis_size("tp")
    row = lax.axis_index("tp")

    def in_copies(i, p, source):
        part = pl.ds(p * rows, rows)
        return (
            pltpu.make_async_copy(g_ref.at[source, part], g_buf.at[i, p], g_sem.at[i, p]),
            pltpu.make_async_copy(m_ref.at[source, part], m_buf.at[i, p], m_sem.at[i, p]),
        )

    def out_copy(i, p):
        return pltpu.make_async_copy(y_buf.at[i, p], outs[i].at[0, pl.ds(p * rows, rows)], y_sem.at[i, p])

    reads = []
    for i, (place_of, c) in enumerate(wanted):
        place = place_of(row) * group + c
        source = jnp.int32(0)
        for j in range(codes_ref.shape[1]):
            source = jnp.where(codes_ref[0, j] == place, j, source)
        for p in range(pieces):
            reads.append((i, p, in_copies(i, p, source)))
            for copy in reads[-1][2]:
                copy.start()
    for i, p, copies in reads:
        for copy in copies:
            copy.wait()
        _, y = nesterov_of(g_buf[i, p], m_buf[i, p])
        y_buf[i, p] = y
        out_copy(i, p).start()
    for i, p, _ in reads:
        out_copy(i, p).wait()


def first_blocks(codes, grads, momentum, wanted, pieces=4):
    _, head, width = grads.shape
    count = len(wanted)
    buffer = pltpu.VMEM((count, pieces, head // pieces, width), jnp.bfloat16)
    return pl.pallas_call(
        functools.partial(first_kernel, wanted, pieces),
        out_shape=[jax.ShapeDtypeStruct((1, head, width), jnp.bfloat16)] * count,
        in_specs=[SMEM, HBM, HBM],
        out_specs=[HBM] * count,
        scratch_shapes=[buffer] * 3 + [pltpu.SemaphoreType.DMA((count, pieces))] * 3,
        name="first_blocks",
    )(codes, grads, momentum)


def all_kernel(spans, spread, tile, source, place, g_ref, m_ref, newm_ref, parts_ref, *refs):
    outs = refs[: len(spans)]
    g_buf, m_buf, v_buf, y_buf, g_sem, m_sem, v_sem, y_sem = refs[len(spans) :]
    blocks, head, width = g_buf.shape
    half = head // 2
    users = blocks // spread

    def in_copies(i):
        return (
            pltpu.make_async_copy(g_ref.at[source[i]], g_buf.at[i], g_sem.at[i]),
            pltpu.make_async_copy(m_ref.at[source[i]], m_buf.at[i], m_sem.at[i]),
        )

    def newm_copy(i):
        return pltpu.make_async_copy(v_buf.at[i], newm_ref.at[source[i]], v_sem.at[i])

    @pl.loop(0, blocks)
    def _(i):
        for copy in in_copies(i):
            copy.start()

    for f in range(users, parts_ref.shape[0]):
        parts_ref[f, : spread * half] = jnp.zeros((spread * half, head), jnp.float32)

    @pl.loop(0, blocks)
    def _(i):
        for copy in in_copies(i):
            copy.wait()
        gram = jnp.zeros((head, head), jnp.float32)
        for k in range(0, width, tile):
            part = pl.ds(k, tile)
            velocity, y = nesterov_of(g_buf[i, :, part], m_buf[i, :, part])
            v_buf[i, :, part] = velocity.astype(jnp.bfloat16)
            y_buf[i, :, part] = y
            gram = gram + lax.dot_general(
                y, y, (((1,), (1,)), ((), ())), preferred_element_type=jnp.float32
            )
        newm_copy(i).start()
        for (start, count), out in zip(spans, outs):

            @pl.when(jnp.logical_and(i >= start, i < start + count))
            def _():
                pltpu.make_async_copy(y_buf.at[i], out.at[i - start], y_sem.at[i]).start()

        to = place[i] // spread
        at = pl.multiple_of(place[i] % spread * half, half)
        parts_ref[to, pl.ds(at, half)] = pack(gram)
        diagonal = diagonal_of(gram)
        for f in range(parts_ref.shape[0]):
            parts_ref[f, pl.ds(spread * half + place[i], 1)] = diagonal

    @pl.loop(0, blocks)
    def _(i):
        newm_copy(i).wait()

    for (start, count), out in zip(spans, outs):
        for k in range(count):
            i = start + k
            pltpu.make_async_copy(y_buf.at[i], out.at[k], y_sem.at[i]).wait()


def all_blocks(source, place, grads, momentum, spans, spread, devices):
    blocks, head, width = grads.shape
    buffer = pltpu.VMEM(grads.shape, jnp.bfloat16)
    return pl.pallas_call(
        functools.partial(all_kernel, spans, spread, min(width, 256)),
        out_shape=[
            jax.ShapeDtypeStruct(grads.shape, jnp.bfloat16),
            jax.ShapeDtypeStruct((devices, spread * head // 2 + blocks, head), jnp.float32),
        ]
        + [jax.ShapeDtypeStruct((count, head, width), jnp.bfloat16) for _, count in spans],
        in_specs=[SMEM, SMEM, HBM, HBM],
        out_specs=[HBM, VMEM] + [HBM] * len(spans),
        scratch_shapes=[buffer] * 4 + [pltpu.SemaphoreType.DMA((blocks,))] * 4,
        name="all_blocks",
    )(source, place, grads, momentum)


def solve_kernel(spread, count, elements, owners, codes, parts_ref, out_ref, slot_ref, sum_ref):
    n_fsdp, _, head = parts_ref.shape
    half = head // 2
    here = lax.axis_index("fsdp")
    total = parts_ref[0]
    for f in range(1, n_fsdp):
        total = total + parts_ref[f]
    diagonals = total[spread * half :]
    squares = jnp.sum(diagonals, axis=1, keepdims=True)
    sum_ref[:count] = diagonals
    sum_ref[count:] = jnp.broadcast_to(jnp.sqrt(squares / elements), (count, head))
    _, lanes = iotas((1, head))
    slots = jnp.zeros((1, head), jnp.float32)
    taken = jnp.int32(0)
    for j in range(count):
        mine = owners[j, 0] == here
        value = sum_ref[pl.ds(count + codes[0, j], 1)]
        slots = slots + jnp.where(jnp.logical_and(mine, lanes == taken), value, 0.0)
        taken = taken + mine.astype(jnp.int32)
    slot_ref[...] = slots

    def dot(a, b):
        return jnp.dot(a, b, precision=lax.Precision.HIGHEST, preferred_element_type=jnp.float32)

    eye_rows, eye_columns = iotas((head, head))
    identity = jnp.where(eye_rows == eye_columns, 1.0, 0.0)
    work = []
    for k in range(spread):
        at = jnp.minimum(here * spread + k, count - 1)
        diagonal = sum_ref[pl.ds(at, 1)]
        inverse = 1.0 / (jnp.sqrt(jnp.sum(diagonal, axis=1, keepdims=True)) + epsilon)
        gram = unpack(total[k * half : (k + 1) * half], diagonal) * (inverse * inverse)
        work.append((inverse, gram, None))
    for i in range(ITERS):
        last = i + 1 == ITERS
        squared = [dot(gram, gram) for _, gram, _ in work]
        mixed = [
            poly_linear * identity + poly_cubic * gram + poly_quintic * s
            for (_, gram, _), s in zip(work, squared)
        ]
        right = [None if last else dot(gram, m) for (_, gram, _), m in zip(work, mixed)]
        turned = [m if q is None else dot(m, q) for (_, _, q), m in zip(work, mixed)]
        grams = [None if last else dot(m, r) for m, r in zip(mixed, right)]
        work = [(inverse, gram, q) for (inverse, _, _), gram, q in zip(work, grams, turned)]
    for k, (inverse, _, q) in enumerate(work):
        q = q * inverse
        out_ref[k * half : (k + 1) * half] = pack(q)
        out_ref[spread * half + k : spread * half + k + 1] = diagonal_of(q)
    rest = out_ref.shape[0] - spread * half - spread
    out_ref[spread * half + spread :] = jnp.zeros((rest, head), jnp.float32)


def solve(parts, owners, codes, spread, elements):
    _, _, head = parts.shape
    count = codes.shape[1]
    return pl.pallas_call(
        functools.partial(solve_kernel, spread, count, elements),
        out_shape=[
            jax.ShapeDtypeStruct((spread * head // 2 + 8 * -(-spread // 8), head), jnp.float32),
            jax.ShapeDtypeStruct((1, head), jnp.float32),
        ],
        in_specs=[SMEM, SMEM, VMEM],
        out_specs=[VMEM, VMEM],
        scratch_shapes=[pltpu.VMEM((2 * count, head), jnp.float32)],
        name="solve",
    )(owners, codes, parts)


def unpack_kernel(spread, packed_ref, out_ref):
    head = packed_ref.shape[2]
    half = head // 2

    @pl.loop(0, out_ref.shape[0] // spread)
    def _(f):
        for k in range(spread):
            packed = packed_ref[f, k * half : (k + 1) * half]
            q = unpack(packed, packed_ref[f, spread * half + k : spread * half + k + 1])
            high = q.astype(jnp.bfloat16)
            out_ref[f * spread + k, :head] = high
            out_ref[f * spread + k, head:] = (q - high.astype(jnp.float32)).astype(jnp.bfloat16)


def unpack_all(packed, spread, blocks):
    head = packed.shape[2]
    return pl.pallas_call(
        functools.partial(unpack_kernel, spread),
        out_shape=jax.ShapeDtypeStruct((blocks, 2 * head, head), jnp.bfloat16),
        in_specs=[VMEM],
        out_specs=VMEM,
        name="unpack_all",
    )(packed)


def apply_kernel(factor, counts, tiles, aliased, place, q_ref, *refs):
    chunks = refs[: len(counts)]
    out = refs[len(counts) + aliased]
    q_buf, y_buf, u_buf, q_sem, y_sem, u_sem = refs[len(counts) + aliased + 1 :]
    head = y_buf.shape[1]
    width = y_buf.shape[2] // tiles
    members = [(chunk, k) for chunk, count in zip(chunks, counts) for k in range(count)]

    def q_copy(i):
        return pltpu.make_async_copy(q_ref.at[place[i]], q_buf.at[i], q_sem.at[i])

    def y_copy(i, j):
        chunk, k = members[i]
        part = pl.ds(j * width, width)
        return pltpu.make_async_copy(chunk.at[k, :, part], y_buf.at[i, :, part], y_sem.at[i, j])

    def u_copy(i, j):
        part = pl.ds(j * width, width)
        return pltpu.make_async_copy(u_buf.at[i, :, part], out.at[place[i], :, part], u_sem.at[i, j])

    for i in range(len(members)):
        q_copy(i).start()
        for j in range(tiles):
            y_copy(i, j).start()
    for i in range(len(members)):
        q_copy(i).wait()
        for j in range(tiles):
            y_copy(i, j).wait()
            part = pl.ds(j * width, width)
            ortho = jnp.dot(q_buf[i], y_buf[i, :, part], preferred_element_type=jnp.float32)
            ortho = ortho[:head] + ortho[head:]
            ortho = ortho.astype(jnp.bfloat16).astype(jnp.float32)
            u_buf[i, :, part] = (-factor * ortho).astype(jnp.bfloat16)
            u_copy(i, j).start()
    for i in range(len(members)):
        for j in range(tiles):
            u_copy(i, j).wait()


def apply_blocks(factor, place, transforms, chunks, into, tiles):
    head, width = chunks[0].shape[1:]
    blocks = transforms.shape[0]
    counts = [chunk.shape[0] for chunk in chunks]
    total = sum(counts)
    in_specs = [SMEM] + [HBM] * (1 + len(chunks))
    operands = [place, transforms, *chunks]
    aliases = {}
    if into is not None:
        aliases = {len(operands): 0}
        in_specs.append(HBM)
        operands.append(into)
    buffer = pltpu.VMEM((total, head, width), jnp.bfloat16)
    copies = pltpu.SemaphoreType.DMA((total, tiles))
    return pl.pallas_call(
        functools.partial(apply_kernel, factor, counts, tiles, len(aliases)),
        out_shape=jax.ShapeDtypeStruct((blocks, head, width), jnp.bfloat16),
        in_specs=in_specs,
        out_specs=HBM,
        scratch_shapes=[
            pltpu.VMEM((total, 2 * head, head), jnp.bfloat16),
            buffer,
            buffer,
            pltpu.SemaphoreType.DMA((total,)),
            copies,
            copies,
        ],
        input_output_aliases=aliases,
        name="apply_blocks",
    )(*operands)


def local(grads, momentum, owner_table, pool_map):
    n_fsdp, n_tp = lax.axis_size("fsdp"), lax.axis_size("tp")
    row = lax.axis_index("tp")
    blocks, head, width = grads.shape
    group = blocks // n_tp
    spread = -(-blocks // n_fsdp)
    paired = n_tp & (n_tp - 1) == 0

    def partner(t, x):
        return t ^ x if paired else (t + x) % n_tp

    def sender(t, x):
        return t ^ x if paired else (t - x) % n_tp

    far = [x for x in range(1, n_tp) if x >= n_tp // 2]
    near = [x for x in range(1, n_tp) if x < n_tp // 2]
    singles = [(x, (c,)) for c in range(group) for x in far]
    held = max(1, len(singles) * 3 // 8)
    first, middle, late = singles[:1], singles[1 : len(singles) - held], singles[len(singles) - held :]
    early = first + [(x, tuple(range(group))) for x in near] + middle
    own = [(0, tuple(range(group)))]
    chunks = early + late + own
    steps = [(x, c) for x, cs in chunks for c in cs]

    codes = pool_map[0]
    position = jnp.arange(blocks, dtype=jnp.int32)
    offsets = jnp.array([c for _, c in steps], jnp.int32)
    partners = jnp.array([x for x, _ in steps], jnp.int32)
    place_out = partner(row, partners) * group + offsets
    place_in = sender(row, partners) * group + offsets
    source = jnp.sum(jnp.where(codes[None, :] == place_out[:, None], position[None, :], 0), axis=1)

    starts, total = {}, 0
    for chunk in chunks:
        starts[chunk] = (total, len(chunk[1]))
        total += len(chunk[1])

    got = {}

    def send(chunk, array):
        got[chunk] = lax.ppermute(array, "tp", [(t, partner(t, chunk[0])) for t in range(n_tp)])

    wanted = [(functools.partial(partner, x=x), cs[0]) for x, cs in first]
    for chunk, array in zip(first, first_blocks(pool_map, grads, momentum, wanted)):
        send(chunk, array)
    rest = chunks[len(first) :]
    new_momentum, parts, *ys = all_blocks(
        source, place_out, grads, momentum, [starts[chunk] for chunk in rest], spread, n_fsdp
    )
    ys = dict(zip(rest, ys))
    for chunk in rest[: -len(own)]:
        send(chunk, ys[chunk])

    parts = lax.all_to_all(parts, "fsdp", split_axis=0, concat_axis=0, tiled=True)
    packed, slots = solve(parts, owner_table, pool_map, spread, head * width * n_fsdp)

    pairs = []
    per_row = group // spread
    for f in range(blocks // spread):
        for t in range(n_tp):
            to = (t * per_row + f % per_row) * n_tp + f // per_row
            pairs.append((f * n_tp + t, to))
    packed = lax.ppermute(packed, ("fsdp", "tp"), pairs)
    packed = jnp.broadcast_to(packed[None], (n_fsdp,) + packed.shape)
    packed = lax.all_to_all(packed, "fsdp", split_axis=0, concat_axis=0, tiled=True)
    transforms = unpack_all(packed, spread, blocks)

    factor = step_size * 0.2 * math.sqrt(width * n_fsdp)
    for chunk in own:
        got[chunk] = ys[chunk]
    update = None
    for members in [own + early] + [[chunk] for chunk in late]:
        where = jnp.concatenate([place_in[s : s + n] for s, n in (starts[chunk] for chunk in members)])
        tiles = 1 if len(members) > 1 or width < 512 else 4
        update = apply_blocks(factor, where, transforms, [got[chunk] for chunk in members], update, tiles)
    return (new_momentum, update, slots[:, :CAP])


def solution(mesh):
    def step(*args):
        return local(*args)

    in_specs = (P("tp", None, "fsdp"), P("tp", None, "fsdp"), P("tp", None), P("tp", None))
    out_specs = (P("tp", None, "fsdp"), P("tp", None, "fsdp"), P("tp", "fsdp"))
    step = jax.shard_map(step, mesh=mesh, in_specs=in_specs, out_specs=out_specs, check_vma=False)
    return step
```

```python
import functools
import math

import jax
import jax.numpy as jnp
from jax import lax
from jax.experimental import pallas as pl
from jax.experimental.pallas import tpu as pltpu
from jax.sharding import PartitionSpec as P


CAP = 2
ITERS = 3

momentum_rate = 0.95
step_size = 0.8
epsilon = 1e-07
poly_linear = 3.4445
poly_cubic = -4.775
poly_quintic = 2.0315


VMEM_BYTES = 67043328
HBM = pl.BlockSpec(memory_space=pltpu.HBM)
SMEM = pl.BlockSpec(memory_space=pltpu.SMEM)
VMEM = pl.BlockSpec(memory_space=pltpu.VMEM)


def nesterov_of(grads, momentum):
    g = grads.astype(jnp.float32)
    velocity = momentum_rate * momentum.astype(jnp.float32) + g
    return velocity, (g + momentum_rate * velocity).astype(jnp.bfloat16)


def iotas(shape):
    return lax.broadcasted_iota(jnp.int32, shape, 0), lax.broadcasted_iota(jnp.int32, shape, 1)


def diagonal_of(square):
    rows, columns = iotas(square.shape)
    return jnp.sum(jnp.where(rows == columns, square, 0.0), axis=0, keepdims=True)


def pack(square):
    half = square.shape[0] // 2
    rows, columns = iotas((half, 2 * half))
    lower = jnp.concatenate([square[half:, half:], square[half:, :half]], axis=1)
    return jnp.where(columns >= rows, square[:half], lower)


def unpack(packed, diagonal):
    half = packed.shape[0]
    rows, columns = iotas(packed.shape)
    top = jnp.where(columns > rows, packed, 0.0)
    turned = jnp.concatenate([packed[:, half:], packed[:, :half]], axis=1)
    keep = jnp.logical_and(columns >= half, columns - half < rows)
    strict = jnp.concatenate([top, jnp.where(keep, turned, 0.0)], axis=0)
    rows, columns = iotas(strict.shape)
    return strict + strict.T + jnp.where(rows == columns, diagonal, 0.0)


def first_kernel(wanted, pieces, codes_ref, g_ref, m_ref, *refs):
    count = len(wanted)
    outs = refs[:count]
    g_buf, m_buf, y_buf, g_sem, m_sem, y_sem = refs[count:]
    rows = g_buf.shape[2]
    group = codes_ref.shape[1] // lax.axis_size("tp")
    row = lax.axis_index("tp")

    def in_copies(i, p, source):
        part = pl.ds(p * rows, rows)
        return (
            pltpu.make_async_copy(g_ref.at[source, part], g_buf.at[i, p], g_sem.at[i, p]),
            pltpu.make_async_copy(m_ref.at[source, part], m_buf.at[i, p], m_sem.at[i, p]),
        )

    def out_copy(i, p):
        return pltpu.make_async_copy(y_buf.at[i, p], outs[i].at[0, pl.ds(p * rows, rows)], y_sem.at[i, p])

    reads = []
    for i, (place_of, c) in enumerate(wanted):
        place = place_of(row) * group + c
        source = jnp.int32(0)
        for j in range(codes_ref.shape[1]):
            source = jnp.where(codes_ref[0, j] == place, j, source)
        for p in range(pieces):
            reads.append((i, p, in_copies(i, p, source)))
            for copy in reads[-1][2]:
                copy.start()
    for i, p, copies in reads:
        for copy in copies:
            copy.wait()
        _, y = nesterov_of(g_buf[i, p], m_buf[i, p])
        y_buf[i, p] = y
        out_copy(i, p).start()
    for i, p, _ in reads:
        out_copy(i, p).wait()


def first_blocks(codes, grads, momentum, wanted, pieces=4):
    _, head, width = grads.shape
    count = len(wanted)
    buffer = pltpu.VMEM((count, pieces, head // pieces, width), jnp.bfloat16)
    return pl.pallas_call(
        functools.partial(first_kernel, wanted, pieces),
        out_shape=[jax.ShapeDtypeStruct((1, head, width), jnp.bfloat16)] * count,
        in_specs=[SMEM, HBM, HBM],
        out_specs=[HBM] * count,
        scratch_shapes=[buffer] * 3 + [pltpu.SemaphoreType.DMA((count, pieces))] * 3,
        name="first_blocks",
    )(codes, grads, momentum)


def all_kernel(spans, spread, tile, source, place, g_ref, m_ref, newm_ref, parts_ref, *refs):
    outs = refs[: len(spans)]
    g_buf, m_buf, v_buf, y_buf, g_sem, m_sem, v_sem, y_sem = refs[len(spans) :]
    blocks, head, width = g_buf.shape
    half = head // 2
    users = blocks // spread

    def in_copies(i):
        return (
            pltpu.make_async_copy(g_ref.at[source[i]], g_buf.at[i], g_sem.at[i]),
            pltpu.make_async_copy(m_ref.at[source[i]], m_buf.at[i], m_sem.at[i]),
        )

    def newm_copy(i):
        return pltpu.make_async_copy(v_buf.at[i], newm_ref.at[source[i]], v_sem.at[i])

    @pl.loop(0, blocks)
    def _(i):
        for copy in in_copies(i):
            copy.start()

    for f in range(users, parts_ref.shape[0]):
        parts_ref[f, : spread * half] = jnp.zeros((spread * half, head), jnp.float32)

    @pl.loop(0, blocks)
    def _(i):
        for copy in in_copies(i):
            copy.wait()
        gram = jnp.zeros((head, head), jnp.float32)
        for k in range(0, width, tile):
            part = pl.ds(k, tile)
            velocity, y = nesterov_of(g_buf[i, :, part], m_buf[i, :, part])
            v_buf[i, :, part] = velocity.astype(jnp.bfloat16)
            y_buf[i, :, part] = y
            gram = gram + lax.dot_general(
                y, y, (((1,), (1,)), ((), ())), preferred_element_type=jnp.float32
            )
        newm_copy(i).start()
        for (start, count), out in zip(spans, outs):

            @pl.when(jnp.logical_and(i >= start, i < start + count))
            def _():
                pltpu.make_async_copy(y_buf.at[i], out.at[i - start], y_sem.at[i]).start()

        to = place[i] // spread
        at = pl.multiple_of(place[i] % spread * half, half)
        parts_ref[to, pl.ds(at, half)] = pack(gram)
        diagonal = diagonal_of(gram)
        for f in range(parts_ref.shape[0]):
            parts_ref[f, pl.ds(spread * half + place[i], 1)] = diagonal

    @pl.loop(0, blocks)
    def _(i):
        newm_copy(i).wait()

    for (start, count), out in zip(spans, outs):
        for k in range(count):
            i = start + k
            pltpu.make_async_copy(y_buf.at[i], out.at[k], y_sem.at[i]).wait()


def all_blocks(source, place, grads, momentum, spans, spread, devices):
    blocks, head, width = grads.shape
    buffer = pltpu.VMEM(grads.shape, jnp.bfloat16)
    return pl.pallas_call(
        functools.partial(all_kernel, spans, spread, min(width, 256)),
        out_shape=[
            jax.ShapeDtypeStruct(grads.shape, jnp.bfloat16),
            jax.ShapeDtypeStruct((devices, spread * head // 2 + blocks, head), jnp.float32),
        ]
        + [jax.ShapeDtypeStruct((count, head, width), jnp.bfloat16) for _, count in spans],
        in_specs=[SMEM, SMEM, HBM, HBM],
        out_specs=[HBM, VMEM] + [HBM] * len(spans),
        scratch_shapes=[buffer] * 4 + [pltpu.SemaphoreType.DMA((blocks,))] * 4,
        name="all_blocks",
    )(source, place, grads, momentum)


def solve_kernel(spread, count, elements, owners, codes, parts_ref, out_ref, slot_ref, sum_ref):
    n_fsdp, _, head = parts_ref.shape
    half = head // 2
    here = lax.axis_index("fsdp")
    total = parts_ref[0]
    for f in range(1, n_fsdp):
        total = total + parts_ref[f]
    diagonals = total[spread * half :]
    squares = jnp.sum(diagonals, axis=1, keepdims=True)
    sum_ref[:count] = diagonals
    sum_ref[count:] = jnp.broadcast_to(jnp.sqrt(squares / elements), (count, head))
    _, lanes = iotas((1, head))
    slots = jnp.zeros((1, head), jnp.float32)
    taken = jnp.int32(0)
    for j in range(count):
        mine = owners[j, 0] == here
        value = sum_ref[pl.ds(count + codes[0, j], 1)]
        slots = slots + jnp.where(jnp.logical_and(mine, lanes == taken), value, 0.0)
        taken = taken + mine.astype(jnp.int32)
    slot_ref[...] = slots

    def dot(a, b):
        return jnp.dot(a, b, precision=lax.Precision.HIGHEST, preferred_element_type=jnp.float32)

    eye_rows, eye_columns = iotas((head, head))
    identity = jnp.where(eye_rows == eye_columns, 1.0, 0.0)
    work = []
    for k in range(spread):
        at = jnp.minimum(here * spread + k, count - 1)
        diagonal = sum_ref[pl.ds(at, 1)]
        inverse = 1.0 / (jnp.sqrt(jnp.sum(diagonal, axis=1, keepdims=True)) + epsilon)
        gram = unpack(total[k * half : (k + 1) * half], diagonal) * (inverse * inverse)
        work.append((inverse, gram, None))
    for i in range(ITERS):
        last = i + 1 == ITERS
        squared = [dot(gram, gram) for _, gram, _ in work]
        mixed = [
            poly_linear * identity + poly_cubic * gram + poly_quintic * s
            for (_, gram, _), s in zip(work, squared)
        ]
        right = [None if last else dot(gram, m) for (_, gram, _), m in zip(work, mixed)]
        turned = [m if q is None else dot(m, q) for (_, _, q), m in zip(work, mixed)]
        grams = [None if last else dot(m, r) for m, r in zip(mixed, right)]
        work = [(inverse, gram, q) for (inverse, _, _), gram, q in zip(work, grams, turned)]
    for k, (inverse, _, q) in enumerate(work):
        q = q * inverse
        out_ref[k * half : (k + 1) * half] = pack(q)
        out_ref[spread * half + k : spread * half + k + 1] = diagonal_of(q)
    rest = out_ref.shape[0] - spread * half - spread
    out_ref[spread * half + spread :] = jnp.zeros((rest, head), jnp.float32)


def solve(parts, owners, codes, spread, elements):
    _, _, head = parts.shape
    count = codes.shape[1]
    return pl.pallas_call(
        functools.partial(solve_kernel, spread, count, elements),
        out_shape=[
            jax.ShapeDtypeStruct((spread * head // 2 + 8 * -(-spread // 8), head), jnp.float32),
            jax.ShapeDtypeStruct((1, head), jnp.float32),
        ],
        in_specs=[SMEM, SMEM, VMEM],
        out_specs=[VMEM, VMEM],
        scratch_shapes=[pltpu.VMEM((2 * count, head), jnp.float32)],
        name="solve",
    )(owners, codes, parts)


def unpack_kernel(spread, packed_ref, out_ref):
    head = packed_ref.shape[2]
    half = head // 2

    @pl.loop(0, out_ref.shape[0] // spread)
    def _(f):
        for k in range(spread):
            packed = packed_ref[f, k * half : (k + 1) * half]
            q = unpack(packed, packed_ref[f, spread * half + k : spread * half + k + 1])
            high = q.astype(jnp.bfloat16)
            out_ref[f * spread + k, :head] = high
            out_ref[f * spread + k, head:] = (q - high.astype(jnp.float32)).astype(jnp.bfloat16)


def unpack_all(packed, spread, blocks):
    head = packed.shape[2]
    return pl.pallas_call(
        functools.partial(unpack_kernel, spread),
        out_shape=jax.ShapeDtypeStruct((blocks, 2 * head, head), jnp.bfloat16),
        in_specs=[VMEM],
        out_specs=VMEM,
        name="unpack_all",
    )(packed)


def apply_kernel(factor, counts, tiles, aliased, place, q_ref, *refs):
    chunks = refs[: len(counts)]
    out = refs[len(counts) + aliased]
    q_buf, y_buf, u_buf, q_sem, y_sem, u_sem = refs[len(counts) + aliased + 1 :]
    head = y_buf.shape[1]
    width = y_buf.shape[2] // tiles
    members = [(chunk, k) for chunk, count in zip(chunks, counts) for k in range(count)]

    def q_copy(i):
        return pltpu.make_async_copy(q_ref.at[place[i]], q_buf.at[i], q_sem.at[i])

    def y_copy(i, j):
        chunk, k = members[i]
        part = pl.ds(j * width, width)
        return pltpu.make_async_copy(chunk.at[k, :, part], y_buf.at[i, :, part], y_sem.at[i, j])

    def u_copy(i, j):
        part = pl.ds(j * width, width)
        return pltpu.make_async_copy(u_buf.at[i, :, part], out.at[place[i], :, part], u_sem.at[i, j])

    for i in range(len(members)):
        q_copy(i).start()
        for j in range(tiles):
            y_copy(i, j).start()
    for i in range(len(members)):
        q_copy(i).wait()
        for j in range(tiles):
            y_copy(i, j).wait()
            part = pl.ds(j * width, width)
            ortho = jnp.dot(q_buf[i], y_buf[i, :, part], preferred_element_type=jnp.float32)
            ortho = ortho[:head] + ortho[head:]
            ortho = ortho.astype(jnp.bfloat16).astype(jnp.float32)
            u_buf[i, :, part] = (-factor * ortho).astype(jnp.bfloat16)
            u_copy(i, j).start()
    for i in range(len(members)):
        for j in range(tiles):
            u_copy(i, j).wait()


def apply_blocks(factor, place, transforms, chunks, into, tiles):
    head, width = chunks[0].shape[1:]
    blocks = transforms.shape[0]
    counts = [chunk.shape[0] for chunk in chunks]
    total = sum(counts)
    in_specs = [SMEM] + [HBM] * (1 + len(chunks))
    operands = [place, transforms, *chunks]
    aliases = {}
    if into is not None:
        aliases = {len(operands): 0}
        in_specs.append(HBM)
        operands.append(into)
    buffer = pltpu.VMEM((total, head, width), jnp.bfloat16)
    copies = pltpu.SemaphoreType.DMA((total, tiles))
    return pl.pallas_call(
        functools.partial(apply_kernel, factor, counts, tiles, len(aliases)),
        out_shape=jax.ShapeDtypeStruct((blocks, head, width), jnp.bfloat16),
        in_specs=in_specs,
        out_specs=HBM,
        scratch_shapes=[
            pltpu.VMEM((total, 2 * head, head), jnp.bfloat16),
            buffer,
            buffer,
            pltpu.SemaphoreType.DMA((total,)),
            copies,
            copies,
        ],
        input_output_aliases=aliases,
        compiler_params=pltpu.CompilerParams(vmem_limit_bytes=VMEM_BYTES),
        name="apply_blocks",
    )(*operands)


def local(grads, momentum, owner_table, pool_map):
    n_fsdp, n_tp = lax.axis_size("fsdp"), lax.axis_size("tp")
    row = lax.axis_index("tp")
    blocks, head, width = grads.shape
    group = blocks // n_tp
    spread = -(-blocks // n_fsdp)
    paired = n_tp & (n_tp - 1) == 0

    def partner(t, x):
        return t ^ x if paired else (t + x) % n_tp

    def sender(t, x):
        return t ^ x if paired else (t - x) % n_tp

    far = [x for x in reversed(range(1, n_tp)) if x >= n_tp // 2]
    near = [x for x in range(1, n_tp) if x < n_tp // 2]
    cut = max(1, group // 2)

    def singles(partners, places):
        return [(x, (c,)) for c in places for x in partners]

    first = singles(far, range(1))
    middle = [chunk for c in range(1, cut) for chunk in singles(near, [c - 1]) + singles(far, [c])]
    early = first + middle
    late = singles(near, range(cut - 1, cut))
    for c in range(cut, group - 1):
        late += singles(far, [c]) + singles(near, [c])
    late += singles(near, [group - 1]) if group > cut else []
    last = singles(far, range(max(cut, group - 1), group))
    late += last
    own = [(0, tuple(range(group)))]
    chunks = early + late + own
    steps = [(x, c) for x, cs in chunks for c in cs]

    codes = pool_map[0]
    position = jnp.arange(blocks, dtype=jnp.int32)
    offsets = jnp.array([c for _, c in steps], jnp.int32)
    partners = jnp.array([x for x, _ in steps], jnp.int32)
    place_out = partner(row, partners) * group + offsets
    place_in = sender(row, partners) * group + offsets
    source = jnp.sum(jnp.where(codes[None, :] == place_out[:, None], position[None, :], 0), axis=1)

    starts, total = {}, 0
    for chunk in chunks:
        starts[chunk] = (total, len(chunk[1]))
        total += len(chunk[1])

    got = {}

    def send(chunk, array):
        got[chunk] = lax.ppermute(array, "tp", [(t, partner(t, chunk[0])) for t in range(n_tp)])

    wanted = [(functools.partial(partner, x=x), cs[0]) for x, cs in first]
    for chunk, array in zip(first, first_blocks(pool_map, grads, momentum, wanted)):
        send(chunk, array)
    rest = chunks[len(first) :]
    new_momentum, parts, *ys = all_blocks(
        source, place_out, grads, momentum, [starts[chunk] for chunk in rest], spread, n_fsdp
    )
    ys = dict(zip(rest, ys))
    for chunk in rest[: -len(own)]:
        send(chunk, ys[chunk])

    parts = lax.all_to_all(parts, "fsdp", split_axis=0, concat_axis=0, tiled=True)
    packed, slots = solve(parts, owner_table, pool_map, spread, head * width * n_fsdp)

    pairs = []
    per_row = group // spread
    for f in range(blocks // spread):
        for t in range(n_tp):
            to = (t * per_row + f % per_row) * n_tp + f // per_row
            pairs.append((f * n_tp + t, to))
    packed = lax.ppermute(packed, ("fsdp", "tp"), pairs)
    packed = jnp.broadcast_to(packed[None], (n_fsdp,) + packed.shape)
    packed = lax.all_to_all(packed, "fsdp", split_axis=0, concat_axis=0, tiled=True)
    transforms = unpack_all(packed, spread, blocks)

    factor = step_size * 0.2 * math.sqrt(width * n_fsdp)
    for chunk in own:
        got[chunk] = ys[chunk]
    update = None
    between = [chunk for chunk in late if chunk not in last]
    rounds = [own + early] + ([between] if between else []) + [[chunk] for chunk in last]
    for members in rounds:
        where = jnp.concatenate([place_in[s : s + n] for s, n in (starts[chunk] for chunk in members)])
        tiles = 1 if len(members) > 1 or width < 512 else 4
        update = apply_blocks(factor, where, transforms, [got[chunk] for chunk in members], update, tiles)
    return (new_momentum, update, slots[:, :CAP])


def solution(mesh):
    def step(*args):
        return local(*args)

    in_specs = (P("tp", None, "fsdp"), P("tp", None, "fsdp"), P("tp", None), P("tp", None))
    out_specs = (P("tp", None, "fsdp"), P("tp", None, "fsdp"), P("tp", "fsdp"))
    step = jax.shard_map(step, mesh=mesh, in_specs=in_specs, out_specs=out_specs, check_vma=False)
    return step
```

```python
import functools
import math

import jax
import jax.numpy as jnp
from jax import lax
from jax.experimental import pallas as pl
from jax.experimental.pallas import tpu as pltpu
from jax.sharding import PartitionSpec as P


CAP = 2
ITERS = 3

momentum_rate = 0.95
step_size = 0.8
epsilon = 1e-07
poly_linear = 3.4445
poly_cubic = -4.775
poly_quintic = 2.0315


VMEM_BYTES = 67043328
HBM = pl.BlockSpec(memory_space=pltpu.HBM)
SMEM = pl.BlockSpec(memory_space=pltpu.SMEM)
VMEM = pl.BlockSpec(memory_space=pltpu.VMEM)


def params(room):
    return pltpu.CompilerParams(vmem_limit_bytes=max(room, 1 << 21))


def params_beside(array):
    return params(VMEM_BYTES - array.size * array.dtype.itemsize * 3 // 4)


def nesterov_of(grads, momentum):
    g = grads.astype(jnp.float32)
    velocity = momentum_rate * momentum.astype(jnp.float32) + g
    return velocity, (g + momentum_rate * velocity).astype(jnp.bfloat16)


def iotas(shape):
    return lax.broadcasted_iota(jnp.int32, shape, 0), lax.broadcasted_iota(jnp.int32, shape, 1)


def diagonal_of(square):
    rows, columns = iotas(square.shape)
    return jnp.sum(jnp.where(rows == columns, square, 0.0), axis=0, keepdims=True)


def pack(square):
    half = square.shape[0] // 2
    rows, columns = iotas((half, 2 * half))
    lower = jnp.concatenate([square[half:, half:], square[half:, :half]], axis=1)
    return jnp.where(columns >= rows, square[:half], lower)


def unpack(packed, diagonal):
    half = packed.shape[0]
    rows, columns = iotas(packed.shape)
    top = jnp.where(columns > rows, packed, 0.0)
    turned = jnp.concatenate([packed[:, half:], packed[:, :half]], axis=1)
    keep = jnp.logical_and(columns >= half, columns - half < rows)
    strict = jnp.concatenate([top, jnp.where(keep, turned, 0.0)], axis=0)
    rows, columns = iotas(strict.shape)
    return strict + strict.T + jnp.where(rows == columns, diagonal, 0.0)


def first_kernel(wanted, pieces, codes_ref, g_ref, m_ref, *refs):
    count = len(wanted)
    outs = refs[:count]
    g_buf, m_buf, g_sem, m_sem = refs[count:]
    rows = g_buf.shape[2]
    group = codes_ref.shape[1] // lax.axis_size("tp")
    row = lax.axis_index("tp")

    def in_copies(i, p, source):
        part = pl.ds(p * rows, rows)
        return (
            pltpu.make_async_copy(g_ref.at[source, part], g_buf.at[i, p], g_sem.at[i, p]),
            pltpu.make_async_copy(m_ref.at[source, part], m_buf.at[i, p], m_sem.at[i, p]),
        )

    reads = []
    for i, (place_of, c) in enumerate(wanted):
        place = place_of(row) * group + c
        source = jnp.int32(0)
        for j in range(codes_ref.shape[1]):
            source = jnp.where(codes_ref[0, j] == place, j, source)
        for p in range(pieces):
            reads.append((i, p, in_copies(i, p, source)))
            for copy in reads[-1][2]:
                copy.start()
    for i, p, copies in reads:
        for copy in copies:
            copy.wait()
        _, y = nesterov_of(g_buf[i, p], m_buf[i, p])
        outs[i][0, p * rows : (p + 1) * rows] = y


def first_blocks(codes, grads, momentum, wanted, pieces=4):
    _, head, width = grads.shape
    count = len(wanted)
    buffer = pltpu.VMEM((count, pieces, head // pieces, width), jnp.bfloat16)
    return pl.pallas_call(
        functools.partial(first_kernel, wanted, pieces),
        out_shape=[jax.ShapeDtypeStruct((1, head, width), jnp.bfloat16)] * count,
        in_specs=[SMEM, HBM, HBM],
        out_specs=[VMEM] * count,
        scratch_shapes=[buffer] * 2 + [pltpu.SemaphoreType.DMA((count, pieces))] * 2,
        compiler_params=params_beside(grads),
        name="first_blocks",
    )(codes, grads, momentum)


def all_kernel(spans, spread, tile, source, place, g_ref, m_ref, newm_ref, parts_ref, *refs):
    outs = refs[: len(spans)]
    g_buf, m_buf, v_buf, y_buf, g_sem, m_sem, v_sem, y_sem = refs[len(spans) :]
    blocks, head, width = g_buf.shape
    half = head // 2
    users = blocks // spread

    def in_copies(i):
        return (
            pltpu.make_async_copy(g_ref.at[source[i]], g_buf.at[i], g_sem.at[i]),
            pltpu.make_async_copy(m_ref.at[source[i]], m_buf.at[i], m_sem.at[i]),
        )

    def newm_copy(i):
        return pltpu.make_async_copy(v_buf.at[i], newm_ref.at[source[i]], v_sem.at[i])

    @pl.loop(0, blocks)
    def _(i):
        for copy in in_copies(i):
            copy.start()

    for f in range(users, parts_ref.shape[0]):
        parts_ref[f, : spread * half] = jnp.zeros((spread * half, head), jnp.float32)

    @pl.loop(0, blocks)
    def _(i):
        for copy in in_copies(i):
            copy.wait()
        gram = jnp.zeros((head, head), jnp.float32)
        for k in range(0, width, tile):
            part = pl.ds(k, tile)
            velocity, y = nesterov_of(g_buf[i, :, part], m_buf[i, :, part])
            v_buf[i, :, part] = velocity.astype(jnp.bfloat16)
            y_buf[i, :, part] = y
            gram = gram + lax.dot_general(
                y, y, (((1,), (1,)), ((), ())), preferred_element_type=jnp.float32
            )
        newm_copy(i).start()
        for (start, count), out in zip(spans, outs):

            @pl.when(jnp.logical_and(i >= start, i < start + count))
            def _():
                pltpu.make_async_copy(y_buf.at[i], out.at[i - start], y_sem.at[i]).start()

        to = place[i] // spread
        at = pl.multiple_of(place[i] % spread * half, half)
        parts_ref[to, pl.ds(at, half)] = pack(gram)
        diagonal = diagonal_of(gram)
        for f in range(parts_ref.shape[0]):
            parts_ref[f, pl.ds(spread * half + place[i], 1)] = diagonal

    @pl.loop(0, blocks)
    def _(i):
        newm_copy(i).wait()

    for (start, count), out in zip(spans, outs):
        for k in range(count):
            i = start + k
            pltpu.make_async_copy(y_buf.at[i], out.at[k], y_sem.at[i]).wait()


def all_blocks(source, place, grads, momentum, spans, spread, devices):
    blocks, head, width = grads.shape
    buffer = pltpu.VMEM(grads.shape, jnp.bfloat16)
    return pl.pallas_call(
        functools.partial(all_kernel, spans, spread, min(width, 256)),
        out_shape=[
            jax.ShapeDtypeStruct(grads.shape, jnp.bfloat16),
            jax.ShapeDtypeStruct((devices, spread * head // 2 + blocks, head), jnp.float32),
        ]
        + [jax.ShapeDtypeStruct((count, head, width), jnp.bfloat16) for _, count in spans],
        in_specs=[SMEM, SMEM, HBM, HBM],
        out_specs=[HBM, VMEM] + [HBM] * len(spans),
        scratch_shapes=[buffer] * 4 + [pltpu.SemaphoreType.DMA((blocks,))] * 4,
        compiler_params=params_beside(grads),
        name="all_blocks",
    )(source, place, grads, momentum)


def solve_kernel(spread, count, elements, owners, codes, parts_ref, out_ref, slot_ref, sum_ref):
    n_fsdp, _, head = parts_ref.shape
    half = head // 2
    here = lax.axis_index("fsdp")
    total = parts_ref[0]
    for f in range(1, n_fsdp):
        total = total + parts_ref[f]
    diagonals = total[spread * half :]
    squares = jnp.sum(diagonals, axis=1, keepdims=True)
    sum_ref[:count] = diagonals
    sum_ref[count:] = jnp.broadcast_to(jnp.sqrt(squares / elements), (count, head))
    _, lanes = iotas((1, head))
    slots = jnp.zeros((1, head), jnp.float32)
    taken = jnp.int32(0)
    for j in range(count):
        mine = owners[j, 0] == here
        value = sum_ref[pl.ds(count + codes[0, j], 1)]
        slots = slots + jnp.where(jnp.logical_and(mine, lanes == taken), value, 0.0)
        taken = taken + mine.astype(jnp.int32)
    slot_ref[...] = slots

    def dot(a, b):
        return jnp.dot(a, b, precision=lax.Precision.HIGHEST, preferred_element_type=jnp.float32)

    eye_rows, eye_columns = iotas((head, head))
    identity = jnp.where(eye_rows == eye_columns, 1.0, 0.0)
    work = []
    for k in range(spread):
        at = jnp.minimum(here * spread + k, count - 1)
        diagonal = sum_ref[pl.ds(at, 1)]
        inverse = 1.0 / (jnp.sqrt(jnp.sum(diagonal, axis=1, keepdims=True)) + epsilon)
        gram = unpack(total[k * half : (k + 1) * half], diagonal) * (inverse * inverse)
        work.append((inverse, gram, None))
    for i in range(ITERS):
        last = i + 1 == ITERS
        squared = [dot(gram, gram) for _, gram, _ in work]
        mixed = [
            poly_linear * identity + poly_cubic * gram + poly_quintic * s
            for (_, gram, _), s in zip(work, squared)
        ]
        right = [None if last else dot(gram, m) for (_, gram, _), m in zip(work, mixed)]
        turned = [m if q is None else dot(m, q) for (_, _, q), m in zip(work, mixed)]
        grams = [None if last else dot(m, r) for m, r in zip(mixed, right)]
        work = [(inverse, gram, q) for (inverse, _, _), gram, q in zip(work, grams, turned)]
    for k, (inverse, _, q) in enumerate(work):
        q = q * inverse
        out_ref[k * half : (k + 1) * half] = pack(q)
        out_ref[spread * half + k : spread * half + k + 1] = diagonal_of(q)
    rest = out_ref.shape[0] - spread * half - spread
    out_ref[spread * half + spread :] = jnp.zeros((rest, head), jnp.float32)


def solve(parts, owners, codes, spread, elements):
    _, _, head = parts.shape
    count = codes.shape[1]
    return pl.pallas_call(
        functools.partial(solve_kernel, spread, count, elements),
        out_shape=[
            jax.ShapeDtypeStruct((spread * head // 2 + 8 * -(-spread // 8), head), jnp.float32),
            jax.ShapeDtypeStruct((1, head), jnp.float32),
        ],
        in_specs=[SMEM, SMEM, VMEM],
        out_specs=[VMEM, VMEM],
        scratch_shapes=[pltpu.VMEM((2 * count, head), jnp.float32)],
        compiler_params=params(4 * parts.size * 4),
        name="solve",
    )(owners, codes, parts)


def unpack_kernel(spread, packed_ref, out_ref):
    head = packed_ref.shape[2]
    half = head // 2

    @pl.loop(0, out_ref.shape[0] // spread)
    def _(f):
        for k in range(spread):
            packed = packed_ref[f, k * half : (k + 1) * half]
            q = unpack(packed, packed_ref[f, spread * half + k : spread * half + k + 1])
            high = q.astype(jnp.bfloat16)
            out_ref[f * spread + k, :head] = high
            out_ref[f * spread + k, head:] = (q - high.astype(jnp.float32)).astype(jnp.bfloat16)


def unpack_all(packed, spread, blocks):
    head = packed.shape[2]
    return pl.pallas_call(
        functools.partial(unpack_kernel, spread),
        out_shape=jax.ShapeDtypeStruct((blocks, 2 * head, head), jnp.bfloat16),
        in_specs=[VMEM],
        out_specs=VMEM,
        compiler_params=params(4 * packed.size * 4),
        name="unpack_all",
    )(packed)


def apply_kernel(factor, counts, tiles, aliased, place, q_ref, *refs):
    chunks = refs[: len(counts)]
    out = refs[len(counts) + aliased]
    u_buf, u_sem = refs[len(counts) + aliased + 1 :]
    head = u_buf.shape[1]
    width = u_buf.shape[2] // tiles
    members = [(chunk, k) for chunk, count in zip(chunks, counts) for k in range(count)]

    def u_copy(i, j):
        part = pl.ds(j * width, width)
        return pltpu.make_async_copy(u_buf.at[i, :, part], out.at[place[i], :, part], u_sem.at[i, j])

    for i, (chunk, k) in enumerate(members):
        q = q_ref[place[i]]
        for j in range(tiles):
            part = pl.ds(j * width, width)
            ortho = jnp.dot(q, chunk[k, :, part], preferred_element_type=jnp.float32)
            ortho = ortho[:head] + ortho[head:]
            ortho = ortho.astype(jnp.bfloat16).astype(jnp.float32)
            u_buf[i, :, part] = (-factor * ortho).astype(jnp.bfloat16)
            u_copy(i, j).start()
    for i in range(len(members)):
        for j in range(tiles):
            u_copy(i, j).wait()


def apply_blocks(factor, place, transforms, chunks, into, tiles):
    head, width = chunks[0].shape[1:]
    blocks = transforms.shape[0]
    counts = [chunk.shape[0] for chunk in chunks]
    total = sum(counts)
    in_specs = [SMEM] + [VMEM] * (1 + len(chunks))
    operands = [place, transforms, *chunks]
    aliases = {}
    if into is not None:
        aliases = {len(operands): 0}
        in_specs.append(HBM)
        operands.append(into)
    return pl.pallas_call(
        functools.partial(apply_kernel, factor, counts, tiles, len(aliases)),
        out_shape=jax.ShapeDtypeStruct((blocks, head, width), jnp.bfloat16),
        in_specs=in_specs,
        out_specs=HBM,
        scratch_shapes=[
            pltpu.VMEM((total, head, width), jnp.bfloat16),
            pltpu.SemaphoreType.DMA((total, tiles)),
        ],
        input_output_aliases=aliases,
        compiler_params=params(4 * total * head * width * 2),
        name="apply_blocks",
    )(*operands)


def local(grads, momentum, owner_table, pool_map):
    n_fsdp, n_tp = lax.axis_size("fsdp"), lax.axis_size("tp")
    row = lax.axis_index("tp")
    blocks, head, width = grads.shape
    group = blocks // n_tp
    spread = -(-blocks // n_fsdp)
    paired = n_tp & (n_tp - 1) == 0

    def partner(t, x):
        return t ^ x if paired else (t + x) % n_tp

    def sender(t, x):
        return t ^ x if paired else (t - x) % n_tp

    far = [x for x in reversed(range(1, n_tp)) if x >= n_tp // 2]
    near = [x for x in range(1, n_tp) if x < n_tp // 2]
    cut = max(1, group // 2)

    def singles(partners, places):
        return [(x, (c,)) for c in places for x in partners]

    first = singles(far, range(1))
    middle = [chunk for c in range(1, cut) for chunk in singles(near, [c - 1]) + singles(far, [c])]
    early = first + middle
    late = singles(near, range(cut - 1, cut))
    for c in range(cut, group - 1):
        late += singles(far, [c]) + singles(near, [c])
    late += singles(near, [group - 1]) if group > cut else []
    last = singles(far, range(max(cut, group - 1), group))
    late += last
    own = [(0, tuple(range(group)))]
    chunks = early + late + own
    steps = [(x, c) for x, cs in chunks for c in cs]

    codes = pool_map[0]
    position = jnp.arange(blocks, dtype=jnp.int32)
    offsets = jnp.array([c for _, c in steps], jnp.int32)
    partners = jnp.array([x for x, _ in steps], jnp.int32)
    place_out = partner(row, partners) * group + offsets
    place_in = sender(row, partners) * group + offsets
    source = jnp.sum(jnp.where(codes[None, :] == place_out[:, None], position[None, :], 0), axis=1)

    starts, total = {}, 0
    for chunk in chunks:
        starts[chunk] = (total, len(chunk[1]))
        total += len(chunk[1])

    got = {}

    def send(chunk, array):
        got[chunk] = lax.ppermute(array, "tp", [(t, partner(t, chunk[0])) for t in range(n_tp)])

    wanted = [(functools.partial(partner, x=x), cs[0]) for x, cs in first]
    for chunk, array in zip(first, first_blocks(pool_map, grads, momentum, wanted)):
        send(chunk, array)
    rest = chunks[len(first) :]
    new_momentum, parts, *ys = all_blocks(
        source, place_out, grads, momentum, [starts[chunk] for chunk in rest], spread, n_fsdp
    )
    ys = dict(zip(rest, ys))
    for chunk in rest[: -len(own)]:
        send(chunk, ys[chunk])

    parts = lax.all_to_all(parts, "fsdp", split_axis=0, concat_axis=0, tiled=True)
    packed, slots = solve(parts, owner_table, pool_map, spread, head * width * n_fsdp)

    pairs = []
    per_row = group // spread
    for f in range(blocks // spread):
        for t in range(n_tp):
            to = (t * per_row + f % per_row) * n_tp + f // per_row
            pairs.append((f * n_tp + t, to))
    packed = lax.ppermute(packed, ("fsdp", "tp"), pairs)
    packed = jnp.broadcast_to(packed[None], (n_fsdp,) + packed.shape)
    packed = lax.all_to_all(packed, "fsdp", split_axis=0, concat_axis=0, tiled=True)
    transforms = unpack_all(packed, spread, blocks)

    factor = step_size * 0.2 * math.sqrt(width * n_fsdp)
    for chunk in own:
        got[chunk] = ys[chunk]
    update = None
    between = [chunk for chunk in late if chunk not in last]
    rounds = [own + early] + ([between] if between else []) + [[chunk] for chunk in last]
    for members in rounds:
        where = jnp.concatenate([place_in[s : s + n] for s, n in (starts[chunk] for chunk in members)])
        tiles = 1 if len(members) > 1 or width < 512 else 4
        update = apply_blocks(factor, where, transforms, [got[chunk] for chunk in members], update, tiles)
    return (new_momentum, update, slots[:, :CAP])


def solution(mesh):
    def step(*args):
        return local(*args)

    in_specs = (P("tp", None, "fsdp"), P("tp", None, "fsdp"), P("tp", None), P("tp", None))
    out_specs = (P("tp", None, "fsdp"), P("tp", None, "fsdp"), P("tp", "fsdp"))
    step = jax.shard_map(step, mesh=mesh, in_specs=in_specs, out_specs=out_specs, check_vma=False)
    return step
```

```python
import functools
import math

import jax
import jax.numpy as jnp
from jax import lax
from jax.experimental import pallas as pl
from jax.experimental.pallas import tpu as pltpu
from jax.sharding import PartitionSpec as P


CAP = 2
ITERS = 3

momentum_rate = 0.95
step_size = 0.8
epsilon = 1e-07
poly_linear = 3.4445
poly_cubic = -4.775
poly_quintic = 2.0315


VMEM_BYTES = 67043328
HBM = pl.BlockSpec(memory_space=pltpu.HBM)
SMEM = pl.BlockSpec(memory_space=pltpu.SMEM)
VMEM = pl.BlockSpec(memory_space=pltpu.VMEM)


def params(room):
    return pltpu.CompilerParams(vmem_limit_bytes=max(room, 1 << 21))


def params_beside(array):
    return params(VMEM_BYTES - array.size * array.dtype.itemsize * 3 // 4)


def nesterov_of(grads, momentum):
    g = grads.astype(jnp.float32)
    velocity = momentum_rate * momentum.astype(jnp.float32) + g
    return velocity, (g + momentum_rate * velocity).astype(jnp.bfloat16)


def iotas(shape):
    return lax.broadcasted_iota(jnp.int32, shape, 0), lax.broadcasted_iota(jnp.int32, shape, 1)


def diagonal_of(square):
    rows, columns = iotas(square.shape)
    return jnp.sum(jnp.where(rows == columns, square, 0.0), axis=0, keepdims=True)


def pack(square):
    half = square.shape[0] // 2
    rows, columns = iotas((half, 2 * half))
    lower = jnp.concatenate([square[half:, half:], square[half:, :half]], axis=1)
    return jnp.where(columns >= rows, square[:half], lower)


def unpack(packed, diagonal):
    half = packed.shape[0]
    rows, columns = iotas(packed.shape)
    top = jnp.where(columns > rows, packed, 0.0)
    turned = jnp.concatenate([packed[:, half:], packed[:, :half]], axis=1)
    keep = jnp.logical_and(columns >= half, columns - half < rows)
    strict = jnp.concatenate([top, jnp.where(keep, turned, 0.0)], axis=0)
    rows, columns = iotas(strict.shape)
    return strict + strict.T + jnp.where(rows == columns, diagonal, 0.0)


def row_of(user, n_tp):
    rank = user % n_tp
    return rank if n_tp % 2 else rank // 2 + rank % 2 * (n_tp // 2)


def user_of(place, spread, per_row, n_tp):
    unit = place // spread
    row, k = unit // per_row, unit % per_row
    rank = row if n_tp % 2 else row % (n_tp // 2) * 2 + row // (n_tp // 2)
    return k * n_tp + rank


def place_of(user, spread, per_row, n_tp):
    return (row_of(user, n_tp) * per_row + user // n_tp) * spread


def first_kernel(wanted, pieces, codes_ref, g_ref, m_ref, *refs):
    count = len(wanted)
    outs = refs[:count]
    g_buf, m_buf, g_sem, m_sem = refs[count:]
    rows = g_buf.shape[2]
    group = codes_ref.shape[1] // lax.axis_size("tp")
    row = lax.axis_index("tp")

    def in_copies(i, p, source):
        part = pl.ds(p * rows, rows)
        return (
            pltpu.make_async_copy(g_ref.at[source, part], g_buf.at[i, p], g_sem.at[i, p]),
            pltpu.make_async_copy(m_ref.at[source, part], m_buf.at[i, p], m_sem.at[i, p]),
        )

    reads = []
    for i, (partner, c) in enumerate(wanted):
        place = partner(row) * group + c
        source = jnp.int32(0)
        for j in range(codes_ref.shape[1]):
            source = jnp.where(codes_ref[0, j] == place, j, source)
        for p in range(pieces):
            reads.append((i, p, in_copies(i, p, source)))
            for copy in reads[-1][2]:
                copy.start()
    for i, p, copies in reads:
        for copy in copies:
            copy.wait()
        _, y = nesterov_of(g_buf[i, p], m_buf[i, p])
        outs[i][0, p * rows : (p + 1) * rows] = y


def first_blocks(codes, grads, momentum, wanted, pieces=4):
    _, head, width = grads.shape
    count = len(wanted)
    buffer = pltpu.VMEM((count, pieces, head // pieces, width), jnp.bfloat16)
    return pl.pallas_call(
        functools.partial(first_kernel, wanted, pieces),
        out_shape=[jax.ShapeDtypeStruct((1, head, width), jnp.bfloat16)] * count,
        in_specs=[SMEM, HBM, HBM],
        out_specs=[VMEM] * count,
        scratch_shapes=[buffer] * 2 + [pltpu.SemaphoreType.DMA((count, pieces))] * 2,
        compiler_params=params_beside(grads),
        name="first_blocks",
    )(codes, grads, momentum)


def all_kernel(spans, spread, tile, source, place, g_ref, m_ref, newm_ref, parts_ref, *refs):
    outs = refs[: len(spans)]
    g_buf, m_buf, v_buf, y_buf, g_sem, m_sem, v_sem, y_sem = refs[len(spans) :]
    blocks, head, width = g_buf.shape
    half = head // 2
    users = blocks // spread
    n_tp = lax.axis_size("tp")
    per_row = users // n_tp

    def in_copies(i):
        return (
            pltpu.make_async_copy(g_ref.at[source[i]], g_buf.at[i], g_sem.at[i]),
            pltpu.make_async_copy(m_ref.at[source[i]], m_buf.at[i], m_sem.at[i]),
        )

    def newm_copy(i):
        return pltpu.make_async_copy(v_buf.at[i], newm_ref.at[source[i]], v_sem.at[i])

    @pl.loop(0, blocks)
    def _(i):
        for copy in in_copies(i):
            copy.start()

    for f in range(users, parts_ref.shape[0]):
        parts_ref[f, : spread * half] = jnp.zeros((spread * half, head), jnp.float32)

    @pl.loop(0, blocks)
    def _(i):
        for copy in in_copies(i):
            copy.wait()
        gram = jnp.zeros((head, head), jnp.float32)
        for k in range(0, width, tile):
            part = pl.ds(k, tile)
            velocity, y = nesterov_of(g_buf[i, :, part], m_buf[i, :, part])
            v_buf[i, :, part] = velocity.astype(jnp.bfloat16)
            y_buf[i, :, part] = y
            gram = gram + lax.dot_general(
                y, y, (((1,), (1,)), ((), ())), preferred_element_type=jnp.float32
            )
        newm_copy(i).start()
        for (start, count), out in zip(spans, outs):

            @pl.when(jnp.logical_and(i >= start, i < start + count))
            def _():
                pltpu.make_async_copy(y_buf.at[i], out.at[i - start], y_sem.at[i]).start()

        to = user_of(place[i], spread, per_row, n_tp)
        at = pl.multiple_of(place[i] % spread * half, half)
        parts_ref[to, pl.ds(at, half)] = pack(gram)
        diagonal = diagonal_of(gram)
        for f in range(parts_ref.shape[0]):
            parts_ref[f, pl.ds(spread * half + place[i], 1)] = diagonal

    @pl.loop(0, blocks)
    def _(i):
        newm_copy(i).wait()

    for (start, count), out in zip(spans, outs):
        for k in range(count):
            i = start + k
            pltpu.make_async_copy(y_buf.at[i], out.at[k], y_sem.at[i]).wait()


def all_blocks(source, place, grads, momentum, spans, spread, devices):
    blocks, head, width = grads.shape
    buffer = pltpu.VMEM(grads.shape, jnp.bfloat16)
    return pl.pallas_call(
        functools.partial(all_kernel, spans, spread, min(width, 256)),
        out_shape=[
            jax.ShapeDtypeStruct(grads.shape, jnp.bfloat16),
            jax.ShapeDtypeStruct((devices, spread * head // 2 + blocks, head), jnp.float32),
        ]
        + [jax.ShapeDtypeStruct((count, head, width), jnp.bfloat16) for _, count in spans],
        in_specs=[SMEM, SMEM, HBM, HBM],
        out_specs=[HBM, VMEM] + [HBM] * len(spans),
        scratch_shapes=[buffer] * 4 + [pltpu.SemaphoreType.DMA((blocks,))] * 4,
        compiler_params=params_beside(grads),
        name="all_blocks",
    )(source, place, grads, momentum)


def solve_kernel(spread, count, elements, owners, codes, parts_ref, out_ref, slot_ref, sum_ref):
    n_fsdp, _, head = parts_ref.shape
    half = head // 2
    here = lax.axis_index("fsdp")
    n_tp = lax.axis_size("tp")
    per_row = count // spread // n_tp
    total = parts_ref[0]
    for f in range(1, n_fsdp):
        total = total + parts_ref[f]
    diagonals = total[spread * half :]
    squares = jnp.sum(diagonals, axis=1, keepdims=True)
    sum_ref[:count] = diagonals
    sum_ref[count:] = jnp.broadcast_to(jnp.sqrt(squares / elements), (count, head))
    _, lanes = iotas((1, head))
    slots = jnp.zeros((1, head), jnp.float32)
    taken = jnp.int32(0)
    for j in range(count):
        mine = owners[j, 0] == here
        value = sum_ref[pl.ds(count + codes[0, j], 1)]
        slots = slots + jnp.where(jnp.logical_and(mine, lanes == taken), value, 0.0)
        taken = taken + mine.astype(jnp.int32)
    slot_ref[...] = slots

    def dot(a, b):
        return jnp.dot(a, b, precision=lax.Precision.HIGHEST, preferred_element_type=jnp.float32)

    eye_rows, eye_columns = iotas((head, head))
    identity = jnp.where(eye_rows == eye_columns, 1.0, 0.0)
    work = []
    for k in range(spread):
        at = jnp.minimum(place_of(here, spread, per_row, n_tp) + k, count - 1)
        diagonal = sum_ref[pl.ds(at, 1)]
        inverse = 1.0 / (jnp.sqrt(jnp.sum(diagonal, axis=1, keepdims=True)) + epsilon)
        gram = unpack(total[k * half : (k + 1) * half], diagonal) * (inverse * inverse)
        work.append((inverse, gram, None))
    for i in range(ITERS):
        last = i + 1 == ITERS
        squared = [dot(gram, gram) for _, gram, _ in work]
        mixed = [
            poly_linear * identity + poly_cubic * gram + poly_quintic * s
            for (_, gram, _), s in zip(work, squared)
        ]
        right = [None if last else dot(gram, m) for (_, gram, _), m in zip(work, mixed)]
        turned = [m if q is None else dot(m, q) for (_, _, q), m in zip(work, mixed)]
        grams = [None if last else dot(m, r) for m, r in zip(mixed, right)]
        work = [(inverse, gram, q) for (inverse, _, _), gram, q in zip(work, grams, turned)]
    for k, (inverse, _, q) in enumerate(work):
        q = q * inverse
        out_ref[k * half : (k + 1) * half] = pack(q)
        out_ref[spread * half + k : spread * half + k + 1] = diagonal_of(q)
    rest = out_ref.shape[0] - spread * half - spread
    out_ref[spread * half + spread :] = jnp.zeros((rest, head), jnp.float32)


def solve(parts, owners, codes, spread, elements):
    _, _, head = parts.shape
    count = codes.shape[1]
    return pl.pallas_call(
        functools.partial(solve_kernel, spread, count, elements),
        out_shape=[
            jax.ShapeDtypeStruct((spread * head // 2 + 8 * -(-spread // 8), head), jnp.float32),
            jax.ShapeDtypeStruct((1, head), jnp.float32),
        ],
        in_specs=[SMEM, SMEM, VMEM],
        out_specs=[VMEM, VMEM],
        scratch_shapes=[pltpu.VMEM((2 * count, head), jnp.float32)],
        compiler_params=params(4 * parts.size * 4),
        name="solve",
    )(owners, codes, parts)


def unpack_kernel(spread, packed_ref, out_ref):
    head = packed_ref.shape[2]
    half = head // 2

    @pl.loop(0, out_ref.shape[0] // spread)
    def _(f):
        for k in range(spread):
            packed = packed_ref[f, k * half : (k + 1) * half]
            q = unpack(packed, packed_ref[f, spread * half + k : spread * half + k + 1])
            high = q.astype(jnp.bfloat16)
            out_ref[f * spread + k, :head] = high
            out_ref[f * spread + k, head:] = (q - high.astype(jnp.float32)).astype(jnp.bfloat16)


def unpack_all(packed, spread, blocks):
    head = packed.shape[2]
    return pl.pallas_call(
        functools.partial(unpack_kernel, spread),
        out_shape=jax.ShapeDtypeStruct((blocks, 2 * head, head), jnp.bfloat16),
        in_specs=[VMEM],
        out_specs=VMEM,
        compiler_params=params(4 * packed.size * 4),
        name="unpack_all",
    )(packed)


def apply_kernel(factor, members, at_end, tiles, q_ref, *refs):
    out = refs[-3]
    u_buf, u_sem = refs[-2:]
    head = u_buf.shape[1]
    width = u_buf.shape[2] // tiles
    row = lax.axis_index("tp")

    def u_copy(i, j):
        part = pl.ds(j * width, width)
        return pltpu.make_async_copy(u_buf.at[i, :, part], out.at[places[i], :, part], u_sem.at[i, j])

    places = [place_at(row) for place_at, _, _ in members]
    for i, (_, ways, k) in enumerate(members):
        q = q_ref[places[i]]
        for j in range(tiles):
            part = pl.ds(j * width, width)
            y = refs[ways[0]][k, :, part]
            if len(ways) > 1:
                y = jnp.where(at_end(row), y, refs[ways[1]][k, :, part])
            ortho = jnp.dot(q, y, preferred_element_type=jnp.float32)
            ortho = ortho[:head] + ortho[head:]
            ortho = ortho.astype(jnp.bfloat16).astype(jnp.float32)
            u_buf[i, :, part] = (-factor * ortho).astype(jnp.bfloat16)
            u_copy(i, j).start()
    for i in range(len(members)):
        for j in range(tiles):
            u_copy(i, j).wait()


def apply_blocks(factor, transforms, chunks, into, at_end, tiles):
    arrays, members = [], []
    for ways, places in chunks:
        at = range(len(arrays), len(arrays) + len(ways))
        arrays += ways
        members += [(place_at, at, k) for k, place_at in enumerate(places)]
    head, width = arrays[0].shape[1:]
    blocks = transforms.shape[0]
    total = len(members)
    in_specs = [VMEM] * (1 + len(arrays))
    operands = [transforms, *arrays]
    aliases = {}
    if into is not None:
        aliases = {len(operands): 0}
        in_specs.append(HBM)
        operands.append(into)
    return pl.pallas_call(
        functools.partial(apply_kernel, factor, members, at_end, tiles),
        out_shape=jax.ShapeDtypeStruct((blocks, head, width), jnp.bfloat16),
        in_specs=in_specs,
        out_specs=HBM,
        scratch_shapes=[
            pltpu.VMEM((total, head, width), jnp.bfloat16),
            pltpu.SemaphoreType.DMA((total, tiles)),
        ],
        input_output_aliases=aliases,
        compiler_params=params(4 * total * head * width * 2),
        name="apply_blocks",
    )(*operands)


def local(grads, momentum, owner_table, pool_map):
    n_fsdp, n_tp = lax.axis_size("fsdp"), lax.axis_size("tp")
    row = lax.axis_index("tp")
    blocks, head, width = grads.shape
    group = blocks // n_tp
    spread = -(-blocks // n_fsdp)
    paired = n_tp & (n_tp - 1) == 0

    def partner(t, x):
        return t ^ x if paired else (t + x) % n_tp

    def sender(t, x):
        return t ^ x if paired else (t - x) % n_tp

    far = [x for x in reversed(range(1, n_tp)) if x >= n_tp // 2]
    near = [x for x in range(1, n_tp) if x < n_tp // 2]
    cut = max(1, group // 2)

    def singles(partners, places):
        return [(x, (c,)) for c in places for x in partners]

    first = singles(far, range(1))
    middle = [chunk for c in range(1, cut) for chunk in singles(near, [c - 1]) + singles(far, [c])]
    early = first + middle
    late = singles(near, range(cut - 1, cut))
    for c in range(cut, group - 1):
        late += singles(far, [c]) + singles(near, [c])
    late += singles(near, [group - 1]) if group > cut else []
    last = singles(far, range(max(cut, group - 1), group))
    late += last
    own = [(0, tuple(range(group)))]
    chunks = early + late + own
    steps = [(x, c) for x, cs in chunks for c in cs]

    codes = pool_map[0]
    position = jnp.arange(blocks, dtype=jnp.int32)
    offsets = jnp.array([c for _, c in steps], jnp.int32)
    partners = jnp.array([x for x, _ in steps], jnp.int32)
    place_out = partner(row, partners) * group + offsets
    source = jnp.sum(jnp.where(codes[None, :] == place_out[:, None], position[None, :], 0), axis=1)

    starts, total = {}, 0
    for chunk in chunks:
        starts[chunk] = (total, len(chunk[1]))
        total += len(chunk[1])

    def at_end(t):
        return jnp.logical_or(t < n_tp // 4, t >= n_tp - n_tp // 4)

    ends = [t for t in range(n_tp) if t < n_tp // 4 or t >= n_tp - n_tp // 4]
    sends = [(chunk, None) for chunk in early + late if chunk not in last]
    if ends:
        sends += [(chunk, side) for side in (0, 1) for chunk in last]
    else:
        sends += [(chunk, None) for chunk in last]
    got = {}

    def send(chunk, side, array):
        pairs = [(t, partner(t, chunk[0])) for t in range(n_tp)]
        if side is not None:
            pairs = [(t, to) for t, to in pairs if (to in ends) == (side == 0)]
        got[chunk, side] = lax.ppermute(array, "tp", pairs)

    wanted = [(functools.partial(partner, x=x), cs[0]) for x, cs in first]
    for chunk, array in zip(first, first_blocks(pool_map, grads, momentum, wanted)):
        send(chunk, None, array)
    rest = chunks[len(first) :]
    new_momentum, parts, *ys = all_blocks(
        source, place_out, grads, momentum, [starts[chunk] for chunk in rest], spread, n_fsdp
    )
    ys = dict(zip(rest, ys))
    for chunk, side in sends[len(first) :]:
        send(chunk, side, ys[chunk])

    parts = lax.all_to_all(parts, "fsdp", split_axis=0, concat_axis=0, tiled=True)
    packed, slots = solve(parts, owner_table, pool_map, spread, head * width * n_fsdp)

    per_row = group // spread
    pairs = []
    for f in range(blocks // spread):
        for t in range(n_tp):
            to = (t * per_row + f // n_tp) * n_tp + row_of(f, n_tp)
            pairs.append((f * n_tp + t, to))
    packed = lax.ppermute(packed, ("fsdp", "tp"), pairs)
    packed = jnp.broadcast_to(packed[None], (n_fsdp,) + packed.shape)
    packed = lax.all_to_all(packed, "fsdp", split_axis=0, concat_axis=0, tiled=True)
    transforms = unpack_all(packed, spread, blocks)

    factor = step_size * 0.2 * math.sqrt(width * n_fsdp)
    for chunk in own:
        got[chunk, None] = ys[chunk]

    def arrival(chunk):
        x, cs = chunk
        ways = [got[chunk, side] for side in (0, 1, None) if (chunk, side) in got]
        return ways, [functools.partial(lambda t, c: sender(t, x) * group + c, c=c) for c in cs]

    update = None
    between = [chunk for chunk in late if chunk not in last]
    for members in [own + early] + ([between] if between else []) + [last]:
        tiles = 1 if len(members) > 2 or width < 512 else 4
        update = apply_blocks(factor, transforms, [arrival(m) for m in members], update, at_end, tiles)
    return (new_momentum, update, slots[:, :CAP])


def solution(mesh):
    def step(*args):
        return local(*args)

    in_specs = (P("tp", None, "fsdp"), P("tp", None, "fsdp"), P("tp", None), P("tp", None))
    out_specs = (P("tp", None, "fsdp"), P("tp", None, "fsdp"), P("tp", "fsdp"))
    step = jax.shard_map(step, mesh=mesh, in_specs=in_specs, out_specs=out_specs, check_vma=False)
    return step
```

```python
import functools
import math

import jax
import jax.numpy as jnp
from jax import lax
from jax.experimental import pallas as pl
from jax.experimental.pallas import tpu as pltpu
from jax.sharding import PartitionSpec as P


CAP = 2
ITERS = 3

momentum_rate = 0.95
step_size = 0.8
epsilon = 1e-07
poly_linear = 3.4445
poly_cubic = -4.775
poly_quintic = 2.0315


VMEM_BYTES = 67043328
HBM = pl.BlockSpec(memory_space=pltpu.HBM)
SMEM = pl.BlockSpec(memory_space=pltpu.SMEM)
VMEM = pl.BlockSpec(memory_space=pltpu.VMEM)


def params(room):
    return pltpu.CompilerParams(vmem_limit_bytes=max(room, 1 << 21))


def params_beside(array):
    return params(VMEM_BYTES - array.size * array.dtype.itemsize * 3 // 4)


def nesterov_of(grads, momentum):
    g = grads.astype(jnp.float32)
    velocity = momentum_rate * momentum.astype(jnp.float32) + g
    return velocity, (g + momentum_rate * velocity).astype(jnp.bfloat16)


def iotas(shape):
    return lax.broadcasted_iota(jnp.int32, shape, 0), lax.broadcasted_iota(jnp.int32, shape, 1)


def diagonal_of(square):
    rows, columns = iotas(square.shape)
    return jnp.sum(jnp.where(rows == columns, square, 0.0), axis=0, keepdims=True)


def pack(square):
    half = square.shape[0] // 2
    rows, columns = iotas((half, 2 * half))
    lower = jnp.concatenate([square[half:, half:], square[half:, :half]], axis=1)
    return jnp.where(columns >= rows, square[:half], lower)


def unpack(packed, diagonal):
    half = packed.shape[0]
    rows, columns = iotas(packed.shape)
    top = jnp.where(columns > rows, packed, 0.0)
    turned = jnp.concatenate([packed[:, half:], packed[:, :half]], axis=1)
    keep = jnp.logical_and(columns >= half, columns - half < rows)
    strict = jnp.concatenate([top, jnp.where(keep, turned, 0.0)], axis=0)
    rows, columns = iotas(strict.shape)
    return strict + strict.T + jnp.where(rows == columns, diagonal, 0.0)


def row_of(user, n_tp):
    rank = user % n_tp
    return rank if n_tp % 2 else rank // 2 + rank % 2 * (n_tp // 2)


def user_of(place, spread, per_row, n_tp):
    unit = place // spread
    row, k = unit // per_row, unit % per_row
    rank = row if n_tp % 2 else row % (n_tp // 2) * 2 + row // (n_tp // 2)
    return k * n_tp + rank


def place_of(user, spread, per_row, n_tp):
    return (row_of(user, n_tp) * per_row + user // n_tp) * spread


def first_kernel(wanted, pieces, codes_ref, g_ref, m_ref, *refs):
    count = len(wanted)
    outs = refs[:count]
    g_buf, m_buf, g_sem, m_sem = refs[count:]
    rows = g_buf.shape[2]
    group = codes_ref.shape[1] // lax.axis_size("tp")
    row = lax.axis_index("tp")

    def in_copies(i, p, source):
        part = pl.ds(p * rows, rows)
        return (
            pltpu.make_async_copy(g_ref.at[source, part], g_buf.at[i, p], g_sem.at[i, p]),
            pltpu.make_async_copy(m_ref.at[source, part], m_buf.at[i, p], m_sem.at[i, p]),
        )

    reads = []
    for i, (partner, c) in enumerate(wanted):
        place = partner(row) * group + c
        source = jnp.int32(0)
        for j in range(codes_ref.shape[1]):
            source = jnp.where(codes_ref[0, j] == place, j, source)
        for p in range(pieces):
            reads.append((i, p, in_copies(i, p, source)))
            for copy in reads[-1][2]:
                copy.start()
    for i, p, copies in reads:
        for copy in copies:
            copy.wait()
        _, y = nesterov_of(g_buf[i, p], m_buf[i, p])
        outs[i][0, p * rows : (p + 1) * rows] = y


def first_blocks(codes, grads, momentum, wanted, pieces=4):
    _, head, width = grads.shape
    count = len(wanted)
    buffer = pltpu.VMEM((count, pieces, head // pieces, width), jnp.bfloat16)
    return pl.pallas_call(
        functools.partial(first_kernel, wanted, pieces),
        out_shape=[pltpu.VMEM((1, head, width), jnp.bfloat16)] * count,
        in_specs=[SMEM, HBM, HBM],
        out_specs=[VMEM] * count,
        scratch_shapes=[buffer] * 2 + [pltpu.SemaphoreType.DMA((count, pieces))] * 2,
        compiler_params=params_beside(grads),
    )(codes, grads, momentum)


def all_kernel(spans, spread, tile, source, place, g_ref, m_ref, newm_ref, parts_ref, *refs):
    outs = refs[: len(spans)]
    g_buf, m_buf, v_buf, y_buf, g_sem, m_sem, v_sem, y_sem = refs[len(spans) :]
    blocks, head, width = g_buf.shape
    half = head // 2
    users = blocks // spread
    n_tp = lax.axis_size("tp")
    per_row = users // n_tp

    def in_copies(i):
        return (
            pltpu.make_async_copy(g_ref.at[source[i]], g_buf.at[i], g_sem.at[i]),
            pltpu.make_async_copy(m_ref.at[source[i]], m_buf.at[i], m_sem.at[i]),
        )

    def newm_copy(i):
        return pltpu.make_async_copy(v_buf.at[i], newm_ref.at[source[i]], v_sem.at[i])

    @pl.loop(0, blocks)
    def _(i):
        for copy in in_copies(i):
            copy.start()

    for f in range(users, parts_ref.shape[0]):
        parts_ref[f, : spread * half] = jnp.zeros((spread * half, head), jnp.float32)

    @pl.loop(0, blocks)
    def _(i):
        for copy in in_copies(i):
            copy.wait()
        gram = jnp.zeros((head, head), jnp.float32)
        for k in range(0, width, tile):
            part = pl.ds(k, tile)
            velocity, y = nesterov_of(g_buf[i, :, part], m_buf[i, :, part])
            v_buf[i, :, part] = velocity.astype(jnp.bfloat16)
            y_buf[i, :, part] = y
            gram = gram + lax.dot_general(
                y, y, (((1,), (1,)), ((), ())), preferred_element_type=jnp.float32
            )
        newm_copy(i).start()
        for (start, count), out in zip(spans, outs):

            @pl.when(jnp.logical_and(i >= start, i < start + count))
            def _():
                pltpu.make_async_copy(y_buf.at[i], out.at[i - start], y_sem.at[i]).start()

        to = user_of(place[i], spread, per_row, n_tp)
        at = pl.multiple_of(place[i] % spread * half, half)
        parts_ref[to, pl.ds(at, half)] = pack(gram)
        diagonal = diagonal_of(gram)
        for f in range(parts_ref.shape[0]):
            parts_ref[f, pl.ds(spread * half + place[i], 1)] = diagonal

    @pl.loop(0, blocks)
    def _(i):
        newm_copy(i).wait()

    for (start, count), out in zip(spans, outs):
        for k in range(count):
            i = start + k
            pltpu.make_async_copy(y_buf.at[i], out.at[k], y_sem.at[i]).wait()


def all_blocks(source, place, grads, momentum, spans, spread, devices):
    blocks, head, width = grads.shape
    buffer = pltpu.VMEM(grads.shape, jnp.bfloat16)
    return pl.pallas_call(
        functools.partial(all_kernel, spans, spread, min(width, 256)),
        out_shape=[
            jax.ShapeDtypeStruct(grads.shape, jnp.bfloat16),
            jax.ShapeDtypeStruct((devices, spread * head // 2 + blocks, head), jnp.float32),
        ]
        + [jax.ShapeDtypeStruct((count, head, width), jnp.bfloat16) for _, count in spans],
        in_specs=[SMEM, SMEM, HBM, HBM],
        out_specs=[HBM, VMEM] + [HBM] * len(spans),
        scratch_shapes=[buffer] * 4 + [pltpu.SemaphoreType.DMA((blocks,))] * 4,
        compiler_params=params_beside(grads),
        name="all_blocks",
    )(source, place, grads, momentum)


def solve_kernel(spread, count, elements, owners, codes, parts_ref, out_ref, slot_ref, sum_ref):
    n_fsdp, _, head = parts_ref.shape
    half = head // 2
    here = lax.axis_index("fsdp")
    n_tp = lax.axis_size("tp")
    per_row = count // spread // n_tp
    total = parts_ref[0]
    for f in range(1, n_fsdp):
        total = total + parts_ref[f]
    diagonals = total[spread * half :]
    squares = jnp.sum(diagonals, axis=1, keepdims=True)
    sum_ref[:count] = diagonals
    sum_ref[count:] = jnp.broadcast_to(jnp.sqrt(squares / elements), (count, head))
    _, lanes = iotas((1, head))
    slots = jnp.zeros((1, head), jnp.float32)
    taken = jnp.int32(0)
    for j in range(count):
        mine = owners[j, 0] == here
        value = sum_ref[pl.ds(count + codes[0, j], 1)]
        slots = slots + jnp.where(jnp.logical_and(mine, lanes == taken), value, 0.0)
        taken = taken + mine.astype(jnp.int32)
    slot_ref[...] = slots

    def dot(a, b):
        return jnp.dot(a, b, precision=lax.Precision.HIGHEST, preferred_element_type=jnp.float32)

    eye_rows, eye_columns = iotas((head, head))
    identity = jnp.where(eye_rows == eye_columns, 1.0, 0.0)
    work = []
    for k in range(spread):
        at = jnp.minimum(place_of(here, spread, per_row, n_tp) + k, count - 1)
        diagonal = sum_ref[pl.ds(at, 1)]
        inverse = 1.0 / (jnp.sqrt(jnp.sum(diagonal, axis=1, keepdims=True)) + epsilon)
        gram = unpack(total[k * half : (k + 1) * half], diagonal) * (inverse * inverse)
        work.append((inverse, gram, None))
    for i in range(ITERS):
        last = i + 1 == ITERS
        squared = [dot(gram, gram) for _, gram, _ in work]
        mixed = [
            poly_linear * identity + poly_cubic * gram + poly_quintic * s
            for (_, gram, _), s in zip(work, squared)
        ]
        right = [None if last else dot(gram, m) for (_, gram, _), m in zip(work, mixed)]
        turned = [m if q is None else dot(m, q) for (_, _, q), m in zip(work, mixed)]
        grams = [None if last else dot(m, r) for m, r in zip(mixed, right)]
        work = [(inverse, gram, q) for (inverse, _, _), gram, q in zip(work, grams, turned)]
    for k, (inverse, _, q) in enumerate(work):
        q = q * inverse
        out_ref[k * half : (k + 1) * half] = pack(q)
        out_ref[spread * half + k : spread * half + k + 1] = diagonal_of(q)
    rest = out_ref.shape[0] - spread * half - spread
    out_ref[spread * half + spread :] = jnp.zeros((rest, head), jnp.float32)


def solve(parts, owners, codes, spread, elements):
    _, _, head = parts.shape
    count = codes.shape[1]
    return pl.pallas_call(
        functools.partial(solve_kernel, spread, count, elements),
        out_shape=[
            jax.ShapeDtypeStruct((spread * head // 2 + 8 * -(-spread // 8), head), jnp.float32),
            jax.ShapeDtypeStruct((1, head), jnp.float32),
        ],
        in_specs=[SMEM, SMEM, VMEM],
        out_specs=[VMEM, VMEM],
        scratch_shapes=[pltpu.VMEM((2 * count, head), jnp.float32)],
        compiler_params=params(4 * parts.size * 4),
        name="solve",
    )(owners, codes, parts)


def unpack_kernel(spread, packed_ref, out_ref):
    head = packed_ref.shape[2]
    half = head // 2

    @pl.loop(0, out_ref.shape[0] // spread)
    def _(f):
        for k in range(spread):
            packed = packed_ref[f, k * half : (k + 1) * half]
            q = unpack(packed, packed_ref[f, spread * half + k : spread * half + k + 1])
            high = q.astype(jnp.bfloat16)
            out_ref[f * spread + k, :head] = high
            out_ref[f * spread + k, head:] = (q - high.astype(jnp.float32)).astype(jnp.bfloat16)


def unpack_all(packed, spread, blocks):
    head = packed.shape[2]
    return pl.pallas_call(
        functools.partial(unpack_kernel, spread),
        out_shape=jax.ShapeDtypeStruct((blocks, 2 * head, head), jnp.bfloat16),
        in_specs=[VMEM],
        out_specs=VMEM,
        compiler_params=params(4 * packed.size * 4),
        name="unpack_all",
    )(packed)


def apply_kernel(factor, members, at_end, tiles, q_ref, *refs):
    out = refs[-3]
    u_buf, u_sem = refs[-2:]
    head = u_buf.shape[1]
    width = u_buf.shape[2] // tiles
    row = lax.axis_index("tp")

    def u_copy(i, j):
        part = pl.ds(j * width, width)
        return pltpu.make_async_copy(u_buf.at[i, :, part], out.at[places[i], :, part], u_sem.at[i, j])

    places = [place_at(row) for place_at, _, _ in members]
    for i, (_, ways, k) in enumerate(members):
        q = q_ref[places[i]]
        for j in range(tiles):
            part = pl.ds(j * width, width)
            y = refs[ways[0]][k, :, part]
            if len(ways) > 1:
                y = jnp.where(at_end(row), y, refs[ways[1]][k, :, part])
            ortho = jnp.dot(q, y, preferred_element_type=jnp.float32)
            ortho = ortho[:head] + ortho[head:]
            ortho = ortho.astype(jnp.bfloat16).astype(jnp.float32)
            u_buf[i, :, part] = (-factor * ortho).astype(jnp.bfloat16)
            u_copy(i, j).start()
    for i in range(len(members)):
        for j in range(tiles):
            u_copy(i, j).wait()


def apply_blocks(factor, transforms, chunks, into, at_end, tiles):
    arrays, members = [], []
    for ways, places in chunks:
        at = range(len(arrays), len(arrays) + len(ways))
        arrays += ways
        members += [(place_at, at, k) for k, place_at in enumerate(places)]
    head, width = arrays[0].shape[1:]
    blocks = transforms.shape[0]
    total = len(members)
    in_specs = [VMEM] * (1 + len(arrays))
    operands = [transforms, *arrays]
    aliases = {}
    if into is not None:
        aliases = {len(operands): 0}
        in_specs.append(HBM)
        operands.append(into)
    return pl.pallas_call(
        functools.partial(apply_kernel, factor, members, at_end, tiles),
        out_shape=jax.ShapeDtypeStruct((blocks, head, width), jnp.bfloat16),
        in_specs=in_specs,
        out_specs=HBM,
        scratch_shapes=[
            pltpu.VMEM((total, head, width), jnp.bfloat16),
            pltpu.SemaphoreType.DMA((total, tiles)),
        ],
        input_output_aliases=aliases,
        compiler_params=params(4 * total * head * width * 2),
        name="apply_blocks",
    )(*operands)


def local(grads, momentum, owner_table, pool_map):
    n_fsdp, n_tp = lax.axis_size("fsdp"), lax.axis_size("tp")
    row = lax.axis_index("tp")
    blocks, head, width = grads.shape
    group = blocks // n_tp
    spread = -(-blocks // n_fsdp)
    paired = n_tp & (n_tp - 1) == 0

    def partner(t, x):
        return t ^ x if paired else (t + x) % n_tp

    def sender(t, x):
        return t ^ x if paired else (t - x) % n_tp

    far = [x for x in reversed(range(1, n_tp)) if x >= n_tp // 2]
    near = [x for x in range(1, n_tp) if x < n_tp // 2]
    cut = max(1, group // 2)

    def singles(partners, places):
        return [(x, (c,)) for c in places for x in partners]

    first = singles(far, range(1))
    middle = [chunk for c in range(1, cut) for chunk in singles(near, [c - 1]) + singles(far, [c])]
    early = first + middle
    late = singles(near, range(cut - 1, cut))
    for c in range(cut, group - 1):
        late += singles(far, [c]) + singles(near, [c])
    late += singles(near, [group - 1]) if group > cut else []
    last = singles(far, range(max(cut, group - 1), group))
    late += last
    own = [(0, tuple(range(group)))]
    chunks = early + late + own
    steps = [(x, c) for x, cs in chunks for c in cs]

    codes = pool_map[0]
    position = jnp.arange(blocks, dtype=jnp.int32)
    offsets = jnp.array([c for _, c in steps], jnp.int32)
    partners = jnp.array([x for x, _ in steps], jnp.int32)
    place_out = partner(row, partners) * group + offsets
    source = jnp.sum(jnp.where(codes[None, :] == place_out[:, None], position[None, :], 0), axis=1)

    starts, total = {}, 0
    for chunk in chunks:
        starts[chunk] = (total, len(chunk[1]))
        total += len(chunk[1])

    def at_end(t):
        return jnp.logical_or(t < n_tp // 4, t >= n_tp - n_tp // 4)

    ends = [t for t in range(n_tp) if t < n_tp // 4 or t >= n_tp - n_tp // 4]
    sends = [(chunk, None) for chunk in early + late if chunk not in last]
    if ends:
        sends += [(chunk, side) for side in (0, 1) for chunk in last]
    else:
        sends += [(chunk, None) for chunk in last]
    got = {}

    def send(chunk, side, array):
        pairs = [(t, partner(t, chunk[0])) for t in range(n_tp)]
        if side is not None:
            pairs = [(t, to) for t, to in pairs if (to in ends) == (side == 0)]
        got[chunk, side] = lax.ppermute(array, "tp", pairs)

    for some in (first[:1], first[1:]):
        wanted = [(functools.partial(partner, x=x), cs[0]) for x, cs in some]
        arrays = first_blocks(pool_map, grads, momentum, wanted) if some else []
        for chunk, array in zip(some, arrays):
            send(chunk, None, array)
    rest = chunks[len(first) :]
    new_momentum, parts, *ys = all_blocks(
        source, place_out, grads, momentum, [starts[chunk] for chunk in rest], spread, n_fsdp
    )
    ys = dict(zip(rest, ys))
    for chunk, side in sends[len(first) :]:
        send(chunk, side, ys[chunk])

    parts = lax.all_to_all(parts, "fsdp", split_axis=0, concat_axis=0, tiled=True)
    packed, slots = solve(parts, owner_table, pool_map, spread, head * width * n_fsdp)

    per_row = group // spread
    pairs = []
    for f in range(blocks // spread):
        for t in range(n_tp):
            to = (t * per_row + f // n_tp) * n_tp + row_of(f, n_tp)
            pairs.append((f * n_tp + t, to))
    packed = lax.ppermute(packed, ("fsdp", "tp"), pairs)
    packed = jnp.broadcast_to(packed[None], (n_fsdp,) + packed.shape)
    packed = lax.all_to_all(packed, "fsdp", split_axis=0, concat_axis=0, tiled=True)
    transforms = unpack_all(packed, spread, blocks)

    factor = step_size * 0.2 * math.sqrt(width * n_fsdp)
    for chunk in own:
        got[chunk, None] = ys[chunk]

    def arrival(chunk):
        x, cs = chunk
        ways = [got[chunk, side] for side in (0, 1, None) if (chunk, side) in got]
        return ways, [functools.partial(lambda t, c: sender(t, x) * group + c, c=c) for c in cs]

    update = None
    between = [chunk for chunk in late if chunk not in last]
    for members in [own + early] + ([between] if between else []) + [last]:
        tiles = 1 if len(members) > 2 or width < 512 else 4
        update = apply_blocks(factor, transforms, [arrival(m) for m in members], update, at_end, tiles)
    return (new_momentum, update, slots[:, :CAP])


def solution(mesh):
    def step(*args):
        return local(*args)

    in_specs = (P("tp", None, "fsdp"), P("tp", None, "fsdp"), P("tp", None), P("tp", None))
    out_specs = (P("tp", None, "fsdp"), P("tp", None, "fsdp"), P("tp", "fsdp"))
    step = jax.shard_map(step, mesh=mesh, in_specs=in_specs, out_specs=out_specs, check_vma=False)
    return step
```

```python
import functools
import math

import jax
import jax.numpy as jnp
from jax import lax
from jax.experimental import pallas as pl
from jax.experimental.pallas import tpu as pltpu
from jax.sharding import PartitionSpec as P


CAP = 2
ITERS = 3

momentum_rate = 0.95
step_size = 0.8
epsilon = 1e-07
poly_linear = 3.4445
poly_cubic = -4.775
poly_quintic = 2.0315


VMEM_BYTES = 67043328
HBM = pl.BlockSpec(memory_space=pltpu.HBM)
SMEM = pl.BlockSpec(memory_space=pltpu.SMEM)
VMEM = pl.BlockSpec(memory_space=pltpu.VMEM)


def params(room):
    return pltpu.CompilerParams(vmem_limit_bytes=max(room, 1 << 21))


def params_beside(array):
    return params(VMEM_BYTES - array.size * array.dtype.itemsize * 3 // 4)


def nesterov_of(grads, momentum):
    g = grads.astype(jnp.float32)
    velocity = momentum_rate * momentum.astype(jnp.float32) + g
    return velocity, (g + momentum_rate * velocity).astype(jnp.bfloat16)


def iotas(shape):
    return lax.broadcasted_iota(jnp.int32, shape, 0), lax.broadcasted_iota(jnp.int32, shape, 1)


def diagonal_of(square):
    rows, columns = iotas(square.shape)
    return jnp.sum(jnp.where(rows == columns, square, 0.0), axis=0, keepdims=True)


def pack(square):
    half = square.shape[0] // 2
    rows, columns = iotas((half, 2 * half))
    lower = jnp.concatenate([square[half:, half:], square[half:, :half]], axis=1)
    return jnp.where(columns >= rows, square[:half], lower)


def unpack(packed, diagonal):
    half = packed.shape[0]
    rows, columns = iotas(packed.shape)
    top = jnp.where(columns > rows, packed, 0.0)
    turned = jnp.concatenate([packed[:, half:], packed[:, :half]], axis=1)
    keep = jnp.logical_and(columns >= half, columns - half < rows)
    strict = jnp.concatenate([top, jnp.where(keep, turned, 0.0)], axis=0)
    rows, columns = iotas(strict.shape)
    return strict + strict.T + jnp.where(rows == columns, diagonal, 0.0)


def row_of(user, n_tp):
    rank = user % n_tp
    return rank if n_tp % 2 else rank // 2 + rank % 2 * (n_tp // 2)


def user_of(place, group, per_row, n_tp):
    row, c = place // group, place % group
    rank = row if n_tp % 2 else row % (n_tp // 2) * 2 + row // (n_tp // 2)
    return c % per_row * n_tp + rank, c // per_row


def place_of(user, slot, group, per_row, n_tp):
    return row_of(user, n_tp) * group + slot * per_row + user // n_tp


def first_kernel(wanted, pieces, codes_ref, g_ref, m_ref, *refs):
    count = len(wanted)
    outs = refs[:count]
    g_buf, m_buf, g_sem, m_sem = refs[count:]
    rows = g_buf.shape[2]
    group = codes_ref.shape[1] // lax.axis_size("tp")
    row = lax.axis_index("tp")

    def in_copies(i, p, source):
        part = pl.ds(p * rows, rows)
        return (
            pltpu.make_async_copy(g_ref.at[source, part], g_buf.at[i, p], g_sem.at[i, p]),
            pltpu.make_async_copy(m_ref.at[source, part], m_buf.at[i, p], m_sem.at[i, p]),
        )

    reads = []
    for i, (partner, c) in enumerate(wanted):
        place = partner(row) * group + c
        source = jnp.int32(0)
        for j in range(codes_ref.shape[1]):
            source = jnp.where(codes_ref[0, j] == place, j, source)
        for p in range(pieces):
            reads.append((i, p, in_copies(i, p, source)))
            for copy in reads[-1][2]:
                copy.start()
    for i, p, copies in reads:
        for copy in copies:
            copy.wait()
        _, y = nesterov_of(g_buf[i, p], m_buf[i, p])
        outs[i][0, p * rows : (p + 1) * rows] = y


def first_blocks(codes, grads, momentum, wanted, pieces=4):
    _, head, width = grads.shape
    count = len(wanted)
    buffer = pltpu.VMEM((count, pieces, head // pieces, width), jnp.bfloat16)
    return pl.pallas_call(
        functools.partial(first_kernel, wanted, pieces),
        out_shape=[pltpu.VMEM((1, head, width), jnp.bfloat16)] * count,
        in_specs=[SMEM, HBM, HBM],
        out_specs=[VMEM] * count,
        scratch_shapes=[buffer] * 2 + [pltpu.SemaphoreType.DMA((count, pieces))] * 2,
        compiler_params=params_beside(grads),
    )(codes, grads, momentum)


def all_kernel(spans, spread, tile, source, place, g_ref, m_ref, newm_ref, parts_ref, *refs):
    outs = refs[: len(spans)]
    g_buf, m_buf, v_buf, y_buf, g_sem, m_sem, v_sem, y_sem = refs[len(spans) :]
    blocks, head, width = g_buf.shape
    half = head // 2
    users = blocks // spread
    n_tp = lax.axis_size("tp")
    per_row = users // n_tp

    def in_copies(i):
        return (
            pltpu.make_async_copy(g_ref.at[source[i]], g_buf.at[i], g_sem.at[i]),
            pltpu.make_async_copy(m_ref.at[source[i]], m_buf.at[i], m_sem.at[i]),
        )

    def newm_copy(i):
        return pltpu.make_async_copy(v_buf.at[i], newm_ref.at[source[i]], v_sem.at[i])

    @pl.loop(0, blocks)
    def _(i):
        for copy in in_copies(i):
            copy.start()

    for f in range(users, parts_ref.shape[0]):
        parts_ref[f, : spread * half] = jnp.zeros((spread * half, head), jnp.float32)

    @pl.loop(0, blocks)
    def _(i):
        for copy in in_copies(i):
            copy.wait()
        gram = jnp.zeros((head, head), jnp.float32)
        for k in range(0, width, tile):
            part = pl.ds(k, tile)
            velocity, y = nesterov_of(g_buf[i, :, part], m_buf[i, :, part])
            v_buf[i, :, part] = velocity.astype(jnp.bfloat16)
            y_buf[i, :, part] = y
            gram = gram + lax.dot_general(
                y, y, (((1,), (1,)), ((), ())), preferred_element_type=jnp.float32
            )
        newm_copy(i).start()
        for (start, count), out in zip(spans, outs):

            @pl.when(jnp.logical_and(i >= start, i < start + count))
            def _():
                pltpu.make_async_copy(y_buf.at[i], out.at[i - start], y_sem.at[i]).start()

        to, slot = user_of(place[i], blocks // n_tp, per_row, n_tp)
        at = pl.multiple_of(slot * half, half)
        parts_ref[to, pl.ds(at, half)] = pack(gram)
        diagonal = diagonal_of(gram)
        for f in range(parts_ref.shape[0]):
            parts_ref[f, pl.ds(spread * half + place[i], 1)] = diagonal

    @pl.loop(0, blocks)
    def _(i):
        newm_copy(i).wait()

    for (start, count), out in zip(spans, outs):
        for k in range(count):
            i = start + k
            pltpu.make_async_copy(y_buf.at[i], out.at[k], y_sem.at[i]).wait()


def all_blocks(source, place, grads, momentum, spans, spread, devices):
    blocks, head, width = grads.shape
    buffer = pltpu.VMEM(grads.shape, jnp.bfloat16)
    return pl.pallas_call(
        functools.partial(all_kernel, spans, spread, min(width, 256)),
        out_shape=[
            jax.ShapeDtypeStruct(grads.shape, jnp.bfloat16),
            jax.ShapeDtypeStruct((devices, spread * head // 2 + blocks, head), jnp.float32),
        ]
        + [jax.ShapeDtypeStruct((count, head, width), jnp.bfloat16) for _, count in spans],
        in_specs=[SMEM, SMEM, HBM, HBM],
        out_specs=[HBM, VMEM] + [HBM] * len(spans),
        scratch_shapes=[buffer] * 4 + [pltpu.SemaphoreType.DMA((blocks,))] * 4,
        compiler_params=params_beside(grads),
        name="all_blocks",
    )(source, place, grads, momentum)


def iterate(work):
    def dot(a, b):
        return jnp.dot(a, b, precision=lax.Precision.HIGHEST, preferred_element_type=jnp.float32)

    head = work[0][0].shape[1]
    rows, columns = iotas((head, head))
    identity = jnp.where(rows == columns, 1.0, 0.0)
    inverses = [1.0 / (jnp.sqrt(jnp.sum(d, axis=1, keepdims=True)) + epsilon) for _, d in work]
    grams = [unpack(p, d) * (inv * inv) for (p, d), inv in zip(work, inverses)]
    turned = [None] * len(work)
    for i in range(ITERS):
        last = i + 1 == ITERS
        squared = [dot(g, g) for g in grams]
        mixed = [poly_linear * identity + poly_cubic * g + poly_quintic * s for g, s in zip(grams, squared)]
        right = [None if last else dot(g, m) for g, m in zip(grams, mixed)]
        turned = [m if q is None else dot(m, q) for q, m in zip(turned, mixed)]
        grams = [None if last else dot(m, r) for m, r in zip(mixed, right)]
    turned = [q * inv for q, inv in zip(turned, inverses)]
    return [(pack(q), diagonal_of(q)) for q in turned]


def write_packed(ref, solved):
    head = ref.shape[1]
    half, count = head // 2, len(solved)
    for k, (packed, diagonal) in enumerate(solved):
        ref[k * half : (k + 1) * half] = packed
        ref[count * half + k : count * half + k + 1] = diagonal
    used = count * half + count
    ref[used:] = jnp.zeros((ref.shape[0] - used, head), jnp.float32)


def packed_rows(count, head):
    return count * head // 2 + 8 * -(-count // 8)


def solve_kernel(spread, skip, count, elements, owners, codes, parts_ref, *refs):
    slot_ref, sum_ref = refs[-2:]
    n_fsdp, _, head = parts_ref.shape
    half = head // 2
    here = lax.axis_index("fsdp")
    n_tp = lax.axis_size("tp")
    per_row = count // spread // n_tp
    total = parts_ref[0]
    for f in range(1, n_fsdp):
        total = total + parts_ref[f]
    diagonals = total[spread * half :]
    squares = jnp.sum(diagonals, axis=1, keepdims=True)
    sum_ref[:count] = diagonals
    sum_ref[count:] = jnp.broadcast_to(jnp.sqrt(squares / elements), (count, head))
    _, lanes = iotas((1, head))
    slots = jnp.zeros((1, head), jnp.float32)
    taken = jnp.int32(0)
    for j in range(count):
        mine = owners[j, 0] == here
        value = sum_ref[pl.ds(count + codes[0, j], 1)]
        slots = slots + jnp.where(jnp.logical_and(mine, lanes == taken), value, 0.0)
        taken = taken + mine.astype(jnp.int32)
    slot_ref[...] = slots

    work = []
    for k in range(spread):
        at = jnp.minimum(place_of(here, k, spread * per_row, per_row, n_tp), count - 1)
        work.append((total[k * half : (k + 1) * half], sum_ref[pl.ds(at, 1)]))
    solved = iterate(work)
    write_packed(refs[0], solved)
    if skip:
        write_packed(refs[1], solved[skip:])


def solve(parts, owners, codes, spread, skip, elements):
    _, _, head = parts.shape
    count = codes.shape[1]
    outs = [packed_rows(spread, head)] + ([packed_rows(spread - skip, head)] if skip else [])
    return pl.pallas_call(
        functools.partial(solve_kernel, spread, skip, count, elements),
        out_shape=[jax.ShapeDtypeStruct((n, head), jnp.float32) for n in outs + [1]],
        in_specs=[SMEM, SMEM, VMEM],
        out_specs=[VMEM] * (len(outs) + 1),
        scratch_shapes=[pltpu.VMEM((2 * count, head), jnp.float32)],
        compiler_params=params(4 * parts.size * 4),
        name="solve",
    )(owners, codes, parts)


def far_kernel(members, per_row, *refs):
    parts_ref = refs[-1]
    head = parts_ref.shape[2]
    half = head // 2
    row = lax.axis_index("tp")
    parts_ref[...] = jnp.zeros(parts_ref.shape, jnp.float32)
    for (source_row, c), ref in zip(members, refs):
        y = ref[0]
        gram = lax.dot_general(y, y, (((1,), (1,)), ((), ())), preferred_element_type=jnp.float32)
        to = source_row(row) * per_row + c
        parts_ref[to, :half] = pack(gram)
        parts_ref[to, half : half + 1] = diagonal_of(gram)


def far_parts(arrays, members, per_row, devices):
    head = arrays[0].shape[1]
    return pl.pallas_call(
        functools.partial(far_kernel, members, per_row),
        out_shape=pltpu.VMEM((devices, packed_rows(1, head), head), jnp.float32),
        in_specs=[VMEM] * len(arrays),
        out_specs=VMEM,
        compiler_params=params(8 * devices * packed_rows(1, head) * head * 4),
        name="far_parts",
    )(*arrays)


def finish_kernel(spread, per_row, parts_ref, same_ref, cross_ref, out_ref):
    n_fsdp, _, head = parts_ref.shape
    half = head // 2
    middle = lax.axis_size("tp") // 2
    source_row = lax.axis_index("fsdp") // per_row
    crossed = (source_row >= middle) != (lax.axis_index("tp") >= middle)
    total = parts_ref[0]
    for f in range(1, n_fsdp):
        total = total + parts_ref[f]
    solved = iterate([(total[:half], total[half : half + 1])])
    sent = spread - 1
    for k in range(sent):
        diagonal = cross_ref[sent * half + k : sent * half + k + 1]
        solved.append((cross_ref[k * half : (k + 1) * half], diagonal))
    chosen = []
    for k, (packed, diagonal) in enumerate(solved):
        other = same_ref[k * half : (k + 1) * half]
        other_diagonal = same_ref[spread * half + k : spread * half + k + 1]
        chosen.append((jnp.where(crossed, packed, other), jnp.where(crossed, diagonal, other_diagonal)))
    write_packed(out_ref, chosen)


def finish(parts, same, cross, spread, per_row):
    return pl.pallas_call(
        functools.partial(finish_kernel, spread, per_row),
        out_shape=jax.ShapeDtypeStruct(same.shape, jnp.float32),
        in_specs=[VMEM] * 3,
        out_specs=VMEM,
        compiler_params=params(8 * parts.size * 4),
        name="finish",
    )(parts, same, cross)


def unpack_kernel(spread, per_row, packed_ref, out_ref):
    head = packed_ref.shape[2]
    half = head // 2

    @pl.loop(0, out_ref.shape[0] // spread)
    def _(f):
        for k in range(spread):
            packed = packed_ref[f, k * half : (k + 1) * half]
            q = unpack(packed, packed_ref[f, spread * half + k : spread * half + k + 1])
            high = q.astype(jnp.bfloat16)
            place = (f // per_row * spread + k) * per_row + f % per_row
            out_ref[place, :, :head] = high
            out_ref[place, :, head:] = (q - high.astype(jnp.float32)).astype(jnp.bfloat16)


def unpack_all(packed, spread, per_row, blocks):
    head = packed.shape[2]
    return pl.pallas_call(
        functools.partial(unpack_kernel, spread, per_row),
        out_shape=jax.ShapeDtypeStruct((blocks, head, 2 * head), jnp.bfloat16),
        in_specs=[VMEM],
        out_specs=VMEM,
        compiler_params=params(4 * packed.size * 4),
        name="unpack_all",
    )(packed)


def apply_kernel(factor, members, at_end, tiles, q_ref, *refs):
    out = refs[-3]
    u_buf, u_sem = refs[-2:]
    width = u_buf.shape[2] // tiles
    row = lax.axis_index("tp")

    def u_copy(i, j):
        part = pl.ds(j * width, width)
        return pltpu.make_async_copy(u_buf.at[i, :, part], out.at[places[i], :, part], u_sem.at[i, j])

    places = [place_at(row) for place_at, _, _ in members]
    for i, (_, ways, k) in enumerate(members):
        q = q_ref[places[i]]
        for j in range(tiles):
            part = pl.ds(j * width, width)
            y = refs[ways[0]][k, :, part]
            if len(ways) > 1:
                y = jnp.where(at_end(row), y, refs[ways[1]][k, :, part])
            y = jnp.concatenate([y, y], axis=0)
            ortho = jnp.dot(q, y, preferred_element_type=jnp.float32)
            ortho = ortho.astype(jnp.bfloat16).astype(jnp.float32)
            u_buf[i, :, part] = (-factor * ortho).astype(jnp.bfloat16)
            u_copy(i, j).start()
    for i in range(len(members)):
        for j in range(tiles):
            u_copy(i, j).wait()


def apply_blocks(factor, transforms, chunks, into, at_end, tiles):
    arrays, members = [], []
    for ways, places in chunks:
        at = range(len(arrays), len(arrays) + len(ways))
        arrays += ways
        members += [(place_at, at, k) for k, place_at in enumerate(places)]
    head, width = arrays[0].shape[1:]
    blocks = transforms.shape[0]
    total = len(members)
    in_specs = [VMEM] * (1 + len(arrays))
    operands = [transforms, *arrays]
    aliases = {}
    if into is not None:
        aliases = {len(operands): 0}
        in_specs.append(HBM)
        operands.append(into)
    return pl.pallas_call(
        functools.partial(apply_kernel, factor, members, at_end, tiles),
        out_shape=jax.ShapeDtypeStruct((blocks, head, width), jnp.bfloat16),
        in_specs=in_specs,
        out_specs=HBM,
        scratch_shapes=[
            pltpu.VMEM((total, head, width), jnp.bfloat16),
            pltpu.SemaphoreType.DMA((total, tiles)),
        ],
        input_output_aliases=aliases,
        compiler_params=params(4 * total * head * width * 2),
        name="apply_blocks",
    )(*operands)


def local(grads, momentum, owner_table, pool_map):
    n_fsdp, n_tp = lax.axis_size("fsdp"), lax.axis_size("tp")
    row = lax.axis_index("tp")
    blocks, head, width = grads.shape
    group = blocks // n_tp
    spread = -(-blocks // n_fsdp)
    paired = n_tp & (n_tp - 1) == 0

    def partner(t, x):
        return t ^ x if paired else (t + x) % n_tp

    def sender(t, x):
        return t ^ x if paired else (t - x) % n_tp

    far = [x for x in reversed(range(1, n_tp)) if x >= n_tp // 2]
    near = [x for x in range(1, n_tp) if x < n_tp // 2]
    cut = max(1, group // 2)

    def singles(partners, places):
        return [(x, (c,)) for c in places for x in partners]

    first = singles(far, range(1))
    early = first + singles(far, range(1, cut)) + singles(near, range(cut - 1))
    late = singles(near, range(cut - 1, cut))
    for c in range(cut, group - 1):
        late += singles(far, [c]) + singles(near, [c])
    late += singles(near, [group - 1]) if group > cut else []
    last = singles(far, range(max(cut, group - 1), group))
    late += last
    own = [(0, tuple(range(group)))]
    chunks = early + late + own
    steps = [(x, c) for x, cs in chunks for c in cs]

    codes = pool_map[0]
    position = jnp.arange(blocks, dtype=jnp.int32)
    offsets = jnp.array([c for _, c in steps], jnp.int32)
    partners = jnp.array([x for x, _ in steps], jnp.int32)
    place_out = partner(row, partners) * group + offsets
    source = jnp.sum(jnp.where(codes[None, :] == place_out[:, None], position[None, :], 0), axis=1)

    starts, total = {}, 0
    for chunk in chunks:
        starts[chunk] = (total, len(chunk[1]))
        total += len(chunk[1])

    def at_end(t):
        return jnp.logical_or(t < n_tp // 4, t >= n_tp - n_tp // 4)

    ends = [t for t in range(n_tp) if t < n_tp // 4 or t >= n_tp - n_tp // 4]
    sends = [(chunk, None) for chunk in early + late if chunk not in last]
    if ends:
        sends += [(chunk, side) for side in (0, 1) for chunk in last]
    else:
        sends += [(chunk, None) for chunk in last]
    got = {}

    def send(chunk, side, array):
        pairs = [(t, partner(t, chunk[0])) for t in range(n_tp)]
        if side is not None:
            pairs = [(t, to) for t, to in pairs if (to in ends) == (side == 0)]
        got[chunk, side] = lax.ppermute(array, "tp", pairs)

    for some in (first[:1], first[1:]):
        wanted = [(functools.partial(partner, x=x), cs[0]) for x, cs in some]
        arrays = first_blocks(pool_map, grads, momentum, wanted) if some else []
        for chunk, array in zip(some, arrays):
            send(chunk, None, array)
    rest = chunks[len(first) :]
    new_momentum, parts, *ys = all_blocks(
        source, place_out, grads, momentum, [starts[chunk] for chunk in rest], spread, n_fsdp
    )
    ys = dict(zip(rest, ys))
    for chunk, side in sends[len(first) :]:
        send(chunk, side, ys[chunk])

    parts = lax.all_to_all(parts, "fsdp", split_axis=0, concat_axis=0, tiled=True)
    per_row = group // spread
    skip = 1 if paired and spread > 1 else 0
    *packed, slots = solve(parts, owner_table, pool_map, spread, skip, head * width * n_fsdp)
    same_pairs, cross_pairs = [], []
    for f in range(blocks // spread):
        for t in range(n_tp):
            row_to = row_of(f, n_tp)
            pair = (f * n_tp + t, (t * per_row + f // n_tp) * n_tp + row_to)
            crosses = skip and (t < n_tp // 2) != (row_to < n_tp // 2)
            (cross_pairs if crosses else same_pairs).append(pair)
    if skip:
        cross = lax.ppermute(packed[1], ("fsdp", "tp"), cross_pairs)
    packed = lax.ppermute(packed[0], ("fsdp", "tp"), same_pairs)
    if skip:
        arrived = singles(far, range(per_row))
        members = [(functools.partial(sender, x=x), cs[0]) for x, cs in arrived]
        parts = far_parts([got[chunk, None] for chunk in arrived], members, per_row, n_fsdp)
        parts, packed, cross = lax.optimization_barrier((parts, packed, cross))
        parts = lax.all_to_all(parts, "fsdp", split_axis=0, concat_axis=0, tiled=True)
        packed = finish(parts, packed, cross, spread, per_row)
    packed = jnp.broadcast_to(packed[None], (n_fsdp,) + packed.shape)
    packed = lax.all_to_all(packed, "fsdp", split_axis=0, concat_axis=0, tiled=True)
    transforms = unpack_all(packed, spread, per_row, blocks)

    factor = step_size * 0.2 * math.sqrt(width * n_fsdp)
    for chunk in own:
        got[chunk, None] = ys[chunk]

    def arrival(chunk):
        x, cs = chunk
        ways = [got[chunk, side] for side in (0, 1, None) if (chunk, side) in got]
        return ways, [functools.partial(lambda t, c: sender(t, x) * group + c, c=c) for c in cs]

    update = None
    between = [chunk for chunk in late if chunk not in last]
    for members in [own + early] + ([between] if between else []) + [last]:
        tiles = 1 if len(members) > 2 or width < 512 else 4
        update = apply_blocks(factor, transforms, [arrival(m) for m in members], update, at_end, tiles)
    return (new_momentum, update, slots[:, :CAP])


def solution(mesh):
    def step(*args):
        return local(*args)

    in_specs = (P("tp", None, "fsdp"), P("tp", None, "fsdp"), P("tp", None), P("tp", None))
    out_specs = (P("tp", None, "fsdp"), P("tp", None, "fsdp"), P("tp", "fsdp"))
    step = jax.shard_map(step, mesh=mesh, in_specs=in_specs, out_specs=out_specs, check_vma=False)
    return step
```

```python
import functools
import math

import jax
import jax.numpy as jnp
from jax import lax
from jax.experimental import pallas as pl
from jax.experimental.pallas import tpu as pltpu
from jax.sharding import PartitionSpec as P


CAP = 2
ITERS = 3

momentum_rate = 0.95
step_size = 0.8
epsilon = 1e-07
poly_linear = 3.4445
poly_cubic = -4.775
poly_quintic = 2.0315


VMEM_BYTES = 67043328
HBM = pl.BlockSpec(memory_space=pltpu.HBM)
SMEM = pl.BlockSpec(memory_space=pltpu.SMEM)
VMEM = pl.BlockSpec(memory_space=pltpu.VMEM)


def params(room):
    return pltpu.CompilerParams(vmem_limit_bytes=max(room, 1 << 21))


def params_beside(array):
    return params(VMEM_BYTES - array.size * array.dtype.itemsize * 3 // 4)


def nesterov_of(grads, momentum):
    g = grads.astype(jnp.float32)
    velocity = momentum_rate * momentum.astype(jnp.float32) + g
    return velocity, (g + momentum_rate * velocity).astype(jnp.bfloat16)


def iotas(shape):
    return lax.broadcasted_iota(jnp.int32, shape, 0), lax.broadcasted_iota(jnp.int32, shape, 1)


def diagonal_of(square):
    rows, columns = iotas(square.shape)
    return jnp.sum(jnp.where(rows == columns, square, 0.0), axis=0, keepdims=True)


def pack(square):
    half = square.shape[0] // 2
    rows, columns = iotas((half, 2 * half))
    lower = jnp.concatenate([square[half:, half:], square[half:, :half]], axis=1)
    return jnp.where(columns >= rows, square[:half], lower)


def unpack(packed, diagonal):
    half = packed.shape[0]
    rows, columns = iotas(packed.shape)
    top = jnp.where(columns > rows, packed, 0.0)
    turned = jnp.concatenate([packed[:, half:], packed[:, :half]], axis=1)
    keep = jnp.logical_and(columns >= half, columns - half < rows)
    strict = jnp.concatenate([top, jnp.where(keep, turned, 0.0)], axis=0)
    rows, columns = iotas(strict.shape)
    return strict + strict.T + jnp.where(rows == columns, diagonal, 0.0)


def row_of(user, n_tp):
    rank = user % n_tp
    return rank if n_tp % 2 else rank // 2 + rank % 2 * (n_tp // 2)


def user_of(place, group, per_row, n_tp):
    row, c = place // group, place % group
    rank = row if n_tp % 2 else row % (n_tp // 2) * 2 + row // (n_tp // 2)
    return c % per_row * n_tp + rank, c // per_row


def place_of(user, slot, group, per_row, n_tp):
    return row_of(user, n_tp) * group + slot * per_row + user // n_tp


def first_kernel(wanted, pieces, codes_ref, g_ref, m_ref, *refs):
    count = len(wanted)
    outs = refs[:count]
    g_buf, m_buf, g_sem, m_sem = refs[count:]
    rows = g_buf.shape[2]
    group = codes_ref.shape[1] // lax.axis_size("tp")
    row = lax.axis_index("tp")

    def in_copies(i, p, source):
        part = pl.ds(p * rows, rows)
        return (
            pltpu.make_async_copy(g_ref.at[source, part], g_buf.at[i, p], g_sem.at[i, p]),
            pltpu.make_async_copy(m_ref.at[source, part], m_buf.at[i, p], m_sem.at[i, p]),
        )

    reads = []
    for i, (partner, c) in enumerate(wanted):
        place = partner(row) * group + c
        source = jnp.int32(0)
        for j in range(codes_ref.shape[1]):
            source = jnp.where(codes_ref[0, j] == place, j, source)
        for p in range(pieces):
            reads.append((i, p, in_copies(i, p, source)))
            for copy in reads[-1][2]:
                copy.start()
    for i, p, copies in reads:
        for copy in copies:
            copy.wait()
        _, y = nesterov_of(g_buf[i, p], m_buf[i, p])
        outs[i][0, p * rows : (p + 1) * rows] = y


def first_blocks(codes, grads, momentum, wanted, pieces=4):
    _, head, width = grads.shape
    count = len(wanted)
    buffer = pltpu.VMEM((count, pieces, head // pieces, width), jnp.bfloat16)
    return pl.pallas_call(
        functools.partial(first_kernel, wanted, pieces),
        out_shape=[pltpu.VMEM((1, head, width), jnp.bfloat16)] * count,
        in_specs=[SMEM, HBM, HBM],
        out_specs=[VMEM] * count,
        scratch_shapes=[buffer] * 2 + [pltpu.SemaphoreType.DMA((count, pieces))] * 2,
        compiler_params=params_beside(grads),
    )(codes, grads, momentum)


def all_kernel(wanted, spans, spread, tile, codes, g_ref, m_ref, newm_ref, parts_ref, *refs):
    outs = refs[: len(spans)]
    g_buf, m_buf, v_buf, y_buf, g_sem, m_sem, v_sem, y_sem, at_place, source, place = refs[len(spans) :]
    blocks, head, width = g_buf.shape
    half = head // 2
    users = blocks // spread
    n_tp = lax.axis_size("tp")
    per_row = users // n_tp

    def in_copies(i):
        return (
            pltpu.make_async_copy(g_ref.at[source[i]], g_buf.at[i], g_sem.at[i]),
            pltpu.make_async_copy(m_ref.at[source[i]], m_buf.at[i], m_sem.at[i]),
        )

    row = lax.axis_index("tp")
    for j in range(blocks):
        at_place[codes[0, j]] = jnp.int32(j)
    for i, (partner, c) in enumerate(wanted):
        place[i] = partner(row) * (blocks // n_tp) + c
        source[i] = at_place[place[i]]

    def newm_copy(i):
        return pltpu.make_async_copy(v_buf.at[i], newm_ref.at[source[i]], v_sem.at[i])

    @pl.loop(0, blocks)
    def _(i):
        for copy in in_copies(i):
            copy.start()

    for f in range(users, parts_ref.shape[0]):
        parts_ref[f, : spread * half] = jnp.zeros((spread * half, head), jnp.float32)

    @pl.loop(0, blocks)
    def _(i):
        for copy in in_copies(i):
            copy.wait()
        gram = jnp.zeros((head, head), jnp.float32)
        for k in range(0, width, tile):
            part = pl.ds(k, tile)
            velocity, y = nesterov_of(g_buf[i, :, part], m_buf[i, :, part])
            v_buf[i, :, part] = velocity.astype(jnp.bfloat16)
            y_buf[i, :, part] = y
            gram = gram + lax.dot_general(
                y, y, (((1,), (1,)), ((), ())), preferred_element_type=jnp.float32
            )
        newm_copy(i).start()
        for (start, count), out in zip(spans, outs):

            @pl.when(jnp.logical_and(i >= start, i < start + count))
            def _():
                pltpu.make_async_copy(y_buf.at[i], out.at[i - start], y_sem.at[i]).start()

        to, slot = user_of(place[i], blocks // n_tp, per_row, n_tp)
        at = pl.multiple_of(slot * half, half)
        parts_ref[to, pl.ds(at, half)] = pack(gram)
        diagonal = diagonal_of(gram)
        for f in range(parts_ref.shape[0]):
            parts_ref[f, pl.ds(spread * half + place[i], 1)] = diagonal

    @pl.loop(0, blocks)
    def _(i):
        newm_copy(i).wait()

    for (start, count), out in zip(spans, outs):
        for k in range(count):
            i = start + k
            pltpu.make_async_copy(y_buf.at[i], out.at[k], y_sem.at[i]).wait()


def all_blocks(codes, grads, momentum, wanted, spans, spread, devices):
    blocks, head, width = grads.shape
    buffer = pltpu.VMEM(grads.shape, jnp.bfloat16)
    return pl.pallas_call(
        functools.partial(all_kernel, wanted, spans, spread, min(width, 256)),
        out_shape=[
            jax.ShapeDtypeStruct(grads.shape, jnp.bfloat16),
            jax.ShapeDtypeStruct((devices, spread * head // 2 + blocks, head), jnp.float32),
        ]
        + [jax.ShapeDtypeStruct((count, head, width), jnp.bfloat16) for _, count in spans],
        in_specs=[SMEM, HBM, HBM],
        out_specs=[HBM, VMEM] + [HBM] * len(spans),
        scratch_shapes=[buffer] * 4
        + [pltpu.SemaphoreType.DMA((blocks,))] * 4
        + [pltpu.SMEM((blocks,), jnp.int32)] * 3,
        compiler_params=params_beside(grads),
        name="all_blocks",
    )(codes, grads, momentum)


def iterate(work):
    def dot(a, b):
        return jnp.dot(a, b, precision=lax.Precision.HIGHEST, preferred_element_type=jnp.float32)

    head = work[0][0].shape[1]
    rows, columns = iotas((head, head))
    identity = jnp.where(rows == columns, 1.0, 0.0)
    inverses = [1.0 / (jnp.sqrt(jnp.sum(d, axis=1, keepdims=True)) + epsilon) for _, d in work]
    grams = [unpack(p, d) * (inv * inv) for (p, d), inv in zip(work, inverses)]
    turned = [None] * len(work)
    for i in range(ITERS):
        last = i + 1 == ITERS
        squared = [dot(g, g) for g in grams]
        mixed = [poly_linear * identity + poly_cubic * g + poly_quintic * s for g, s in zip(grams, squared)]
        right = [None if last else dot(g, m) for g, m in zip(grams, mixed)]
        turned = [m if q is None else dot(m, q) for q, m in zip(turned, mixed)]
        grams = [None if last else dot(m, r) for m, r in zip(mixed, right)]
    turned = [q * inv for q, inv in zip(turned, inverses)]
    return [(pack(q), diagonal_of(q)) for q in turned]


def write_packed(ref, solved):
    head = ref.shape[1]
    half, count = head // 2, len(solved)
    for k, (packed, diagonal) in enumerate(solved):
        ref[k * half : (k + 1) * half] = packed
        ref[count * half + k : count * half + k + 1] = diagonal
    used = count * half + count
    ref[used:] = jnp.zeros((ref.shape[0] - used, head), jnp.float32)


def packed_rows(count, head):
    return count * head // 2 + 8 * -(-count // 8)


def solve_kernel(spread, skip, count, elements, owners, codes, parts_ref, *refs):
    slot_ref, sum_ref = refs[-2:]
    n_fsdp, _, head = parts_ref.shape
    half = head // 2
    here = lax.axis_index("fsdp")
    n_tp = lax.axis_size("tp")
    per_row = count // spread // n_tp
    total = parts_ref[0]
    for f in range(1, n_fsdp):
        total = total + parts_ref[f]
    diagonals = total[spread * half :]
    squares = jnp.sum(diagonals, axis=1, keepdims=True)
    sum_ref[:count] = diagonals
    sum_ref[count:] = jnp.broadcast_to(jnp.sqrt(squares / elements), (count, head))
    _, lanes = iotas((1, head))
    slots = jnp.zeros((1, head), jnp.float32)
    taken = jnp.int32(0)
    for j in range(count):
        mine = owners[j, 0] == here
        value = sum_ref[pl.ds(count + codes[0, j], 1)]
        slots = slots + jnp.where(jnp.logical_and(mine, lanes == taken), value, 0.0)
        taken = taken + mine.astype(jnp.int32)
    slot_ref[...] = slots

    work = []
    for k in range(spread):
        at = jnp.minimum(place_of(here, k, spread * per_row, per_row, n_tp), count - 1)
        work.append((total[k * half : (k + 1) * half], sum_ref[pl.ds(at, 1)]))
    solved = iterate(work)
    write_packed(refs[0], solved)
    if skip:
        write_packed(refs[1], solved[skip:])


def solve(parts, owners, codes, spread, skip, elements):
    _, _, head = parts.shape
    count = codes.shape[1]
    outs = [packed_rows(spread, head)] + ([packed_rows(spread - skip, head)] if skip else [])
    return pl.pallas_call(
        functools.partial(solve_kernel, spread, skip, count, elements),
        out_shape=[jax.ShapeDtypeStruct((n, head), jnp.float32) for n in outs + [1]],
        in_specs=[SMEM, SMEM, VMEM],
        out_specs=[VMEM] * (len(outs) + 1),
        scratch_shapes=[pltpu.VMEM((2 * count, head), jnp.float32)],
        compiler_params=params(4 * parts.size * 4),
        name="solve",
    )(owners, codes, parts)


def far_kernel(members, per_row, *refs):
    parts_ref = refs[-1]
    head = parts_ref.shape[2]
    half = head // 2
    row = lax.axis_index("tp")
    parts_ref[...] = jnp.zeros(parts_ref.shape, jnp.float32)
    for (source_row, c), ref in zip(members, refs):
        y = ref[0]
        gram = lax.dot_general(y, y, (((1,), (1,)), ((), ())), preferred_element_type=jnp.float32)
        to = source_row(row) * per_row + c
        parts_ref[to, :half] = pack(gram)
        parts_ref[to, half : half + 1] = diagonal_of(gram)


def far_parts(arrays, members, per_row, devices):
    head = arrays[0].shape[1]
    return pl.pallas_call(
        functools.partial(far_kernel, members, per_row),
        out_shape=pltpu.VMEM((devices, packed_rows(1, head), head), jnp.float32),
        in_specs=[VMEM] * len(arrays),
        out_specs=VMEM,
        compiler_params=params(8 * devices * packed_rows(1, head) * head * 4),
        name="far_parts",
    )(*arrays)


def finish_kernel(spread, per_row, parts_ref, same_ref, cross_ref, out_ref):
    n_fsdp, _, head = parts_ref.shape
    half = head // 2
    middle = lax.axis_size("tp") // 2
    source_row = lax.axis_index("fsdp") // per_row
    crossed = (source_row >= middle) != (lax.axis_index("tp") >= middle)
    total = parts_ref[0]
    for f in range(1, n_fsdp):
        total = total + parts_ref[f]
    solved = iterate([(total[:half], total[half : half + 1])])
    sent = spread - 1
    for k in range(sent):
        diagonal = cross_ref[sent * half + k : sent * half + k + 1]
        solved.append((cross_ref[k * half : (k + 1) * half], diagonal))
    chosen = []
    for k, (packed, diagonal) in enumerate(solved):
        other = same_ref[k * half : (k + 1) * half]
        other_diagonal = same_ref[spread * half + k : spread * half + k + 1]
        chosen.append((jnp.where(crossed, packed, other), jnp.where(crossed, diagonal, other_diagonal)))
    write_packed(out_ref, chosen)


def finish(parts, same, cross, spread, per_row):
    return pl.pallas_call(
        functools.partial(finish_kernel, spread, per_row),
        out_shape=jax.ShapeDtypeStruct(same.shape, jnp.float32),
        in_specs=[VMEM] * 3,
        out_specs=VMEM,
        compiler_params=params(8 * parts.size * 4),
        name="finish",
    )(parts, same, cross)


def unpack_kernel(spread, per_row, packed_ref, out_ref):
    head = packed_ref.shape[2]
    half = head // 2

    @pl.loop(0, out_ref.shape[0] // spread)
    def _(f):
        for k in range(spread):
            packed = packed_ref[f, k * half : (k + 1) * half]
            q = unpack(packed, packed_ref[f, spread * half + k : spread * half + k + 1])
            high = q.astype(jnp.bfloat16)
            place = (f // per_row * spread + k) * per_row + f % per_row
            out_ref[place, :, :head] = high
            out_ref[place, :, head:] = (q - high.astype(jnp.float32)).astype(jnp.bfloat16)


def unpack_all(packed, spread, per_row, blocks):
    head = packed.shape[2]
    return pl.pallas_call(
        functools.partial(unpack_kernel, spread, per_row),
        out_shape=jax.ShapeDtypeStruct((blocks, head, 2 * head), jnp.bfloat16),
        in_specs=[VMEM],
        out_specs=VMEM,
        compiler_params=params(4 * packed.size * 4),
        name="unpack_all",
    )(packed)


def apply_kernel(factor, members, at_end, tiles, q_ref, *refs):
    out = refs[-3]
    u_buf, u_sem = refs[-2:]
    width = u_buf.shape[2] // tiles
    row = lax.axis_index("tp")

    def u_copy(i, j):
        part = pl.ds(j * width, width)
        return pltpu.make_async_copy(u_buf.at[i, :, part], out.at[places[i], :, part], u_sem.at[i, j])

    places = [place_at(row) for place_at, _, _ in members]
    for i, (_, ways, k) in enumerate(members):
        q = q_ref[places[i]]
        for j in range(tiles):
            part = pl.ds(j * width, width)
            y = refs[ways[0]][k, :, part]
            if len(ways) > 1:
                y = jnp.where(at_end(row), y, refs[ways[1]][k, :, part])
            y = jnp.concatenate([y, y], axis=0)
            ortho = jnp.dot(q, y, preferred_element_type=jnp.float32)
            ortho = ortho.astype(jnp.bfloat16).astype(jnp.float32)
            u_buf[i, :, part] = (-factor * ortho).astype(jnp.bfloat16)
            u_copy(i, j).start()
    for i in range(len(members)):
        for j in range(tiles):
            u_copy(i, j).wait()


def apply_blocks(factor, transforms, chunks, into, at_end, tiles):
    arrays, members = [], []
    for ways, places in chunks:
        at = range(len(arrays), len(arrays) + len(ways))
        arrays += ways
        members += [(place_at, at, k) for k, place_at in enumerate(places)]
    head, width = arrays[0].shape[1:]
    blocks = transforms.shape[0]
    total = len(members)
    in_specs = [VMEM] * (1 + len(arrays))
    operands = [transforms, *arrays]
    aliases = {}
    if into is not None:
        aliases = {len(operands): 0}
        in_specs.append(HBM)
        operands.append(into)
    return pl.pallas_call(
        functools.partial(apply_kernel, factor, members, at_end, tiles),
        out_shape=jax.ShapeDtypeStruct((blocks, head, width), jnp.bfloat16),
        in_specs=in_specs,
        out_specs=HBM,
        scratch_shapes=[
            pltpu.VMEM((total, head, width), jnp.bfloat16),
            pltpu.SemaphoreType.DMA((total, tiles)),
        ],
        input_output_aliases=aliases,
        compiler_params=params(4 * total * head * width * 2),
        name="apply_blocks",
    )(*operands)


def local(grads, momentum, owner_table, pool_map):
    n_fsdp, n_tp = lax.axis_size("fsdp"), lax.axis_size("tp")
    blocks, head, width = grads.shape
    group = blocks // n_tp
    spread = -(-blocks // n_fsdp)
    paired = n_tp & (n_tp - 1) == 0

    def partner(t, x):
        return t ^ x if paired else (t + x) % n_tp

    def sender(t, x):
        return t ^ x if paired else (t - x) % n_tp

    far = [x for x in reversed(range(1, n_tp)) if x >= n_tp // 2]
    near = [x for x in range(1, n_tp) if x < n_tp // 2]
    cut = max(1, group // 2)

    def singles(partners, places):
        return [(x, (c,)) for c in places for x in partners]

    first = singles(far, range(1))
    early = first + singles(far, range(1, cut)) + singles(near, range(cut - 1))
    late = []
    for c in range(cut, group - 1):
        late += singles(far, [c]) + singles(near, [c - 1, c])
    late += singles(near, [group - 1]) if group > cut else []
    last = singles(far, range(max(cut, group - 1), group))
    late += last
    own = [(0, tuple(range(group)))]
    chunks = early + late + own
    steps = [(x, c) for x, cs in chunks for c in cs]

    starts, total = {}, 0
    for chunk in chunks:
        starts[chunk] = (total, len(chunk[1]))
        total += len(chunk[1])

    def at_end(t):
        return jnp.logical_or(t < n_tp // 4, t >= n_tp - n_tp // 4)

    ends = [t for t in range(n_tp) if t < n_tp // 4 or t >= n_tp - n_tp // 4]
    sends = [(chunk, None) for chunk in early + late if chunk not in last]
    if ends:
        sends += [(chunk, side) for side in (0, 1) for chunk in last]
    else:
        sends += [(chunk, None) for chunk in last]
    got = {}

    def send(chunk, side, array):
        pairs = [(t, partner(t, chunk[0])) for t in range(n_tp)]
        if side is not None:
            pairs = [(t, to) for t, to in pairs if (to in ends) == (side == 0)]
        got[chunk, side] = lax.ppermute(array, "tp", pairs)

    for some in (first[:1], first[1:]):
        wanted = [(functools.partial(partner, x=x), cs[0]) for x, cs in some]
        arrays = first_blocks(pool_map, grads, momentum, wanted) if some else []
        for chunk, array in zip(some, arrays):
            send(chunk, None, array)
    rest = chunks[len(first) :]
    order = [(functools.partial(partner, x=x), c) for x, c in steps]
    new_momentum, parts, *ys = all_blocks(
        pool_map, grads, momentum, order, [starts[chunk] for chunk in rest], spread, n_fsdp
    )
    ys = dict(zip(rest, ys))
    for chunk, side in sends[len(first) :]:
        send(chunk, side, ys[chunk])

    parts = lax.all_to_all(parts, "fsdp", split_axis=0, concat_axis=0, tiled=True)
    per_row = group // spread
    skip = 1 if paired and spread > 1 else 0
    *packed, slots = solve(parts, owner_table, pool_map, spread, skip, head * width * n_fsdp)
    same_pairs, cross_pairs = [], []
    for f in range(blocks // spread):
        for t in range(n_tp):
            row_to = row_of(f, n_tp)
            pair = (f * n_tp + t, (t * per_row + f // n_tp) * n_tp + row_to)
            crosses = skip and (t < n_tp // 2) != (row_to < n_tp // 2)
            (cross_pairs if crosses else same_pairs).append(pair)
    if skip:
        cross = lax.ppermute(packed[1], ("fsdp", "tp"), cross_pairs)
    packed = lax.ppermute(packed[0], ("fsdp", "tp"), same_pairs)
    if skip:
        arrived = singles(far, range(per_row))
        members = [(functools.partial(sender, x=x), cs[0]) for x, cs in arrived]
        parts = far_parts([got[chunk, None] for chunk in arrived], members, per_row, n_fsdp)
        parts, packed, cross = lax.optimization_barrier((parts, packed, cross))
        parts = lax.all_to_all(parts, "fsdp", split_axis=0, concat_axis=0, tiled=True)
        packed = finish(parts, packed, cross, spread, per_row)
    packed = jnp.broadcast_to(packed[None], (n_fsdp,) + packed.shape)
    packed = lax.all_to_all(packed, "fsdp", split_axis=0, concat_axis=0, tiled=True)
    transforms = unpack_all(packed, spread, per_row, blocks)

    factor = step_size * 0.2 * math.sqrt(width * n_fsdp)
    for chunk in own:
        got[chunk, None] = ys[chunk]

    def arrival(chunk):
        x, cs = chunk
        ways = [got[chunk, side] for side in (0, 1, None) if (chunk, side) in got]
        return ways, [functools.partial(lambda t, c: sender(t, x) * group + c, c=c) for c in cs]

    update = None
    between = [chunk for chunk in late if chunk not in last]
    for members in [own + early] + ([between] if between else []) + [last]:
        tiles = 1 if len(members) > 2 or width < 512 else 4
        update = apply_blocks(factor, transforms, [arrival(m) for m in members], update, at_end, tiles)
    return (new_momentum, update, slots[:, :CAP])


def solution(mesh):
    def step(*args):
        return local(*args)

    in_specs = (P("tp", None, "fsdp"), P("tp", None, "fsdp"), P("tp", None), P("tp", None))
    out_specs = (P("tp", None, "fsdp"), P("tp", None, "fsdp"), P("tp", "fsdp"))
    step = jax.shard_map(step, mesh=mesh, in_specs=in_specs, out_specs=out_specs, check_vma=False)
    return step
```

```python
import functools
import math

import jax
import jax.numpy as jnp
from jax import lax
from jax.experimental import pallas as pl
from jax.experimental.pallas import tpu as pltpu
from jax.sharding import PartitionSpec as P


CAP = 2
ITERS = 3

momentum_rate = 0.95
step_size = 0.8
epsilon = 1e-07
poly_linear = 3.4445
poly_cubic = -4.775
poly_quintic = 2.0315


VMEM_BYTES = 67043328
HBM = pl.BlockSpec(memory_space=pltpu.HBM)
SMEM = pl.BlockSpec(memory_space=pltpu.SMEM)
VMEM = pl.BlockSpec(memory_space=pltpu.VMEM)


def params(room):
    return pltpu.CompilerParams(vmem_limit_bytes=max(room, 1 << 21))


def params_beside(array):
    return params(VMEM_BYTES - array.size * array.dtype.itemsize * 3 // 4)


def nesterov_of(grads, momentum):
    g = grads.astype(jnp.float32)
    velocity = momentum_rate * momentum.astype(jnp.float32) + g
    return velocity, (g + momentum_rate * velocity).astype(jnp.bfloat16)


def iotas(shape):
    return lax.broadcasted_iota(jnp.int32, shape, 0), lax.broadcasted_iota(jnp.int32, shape, 1)


def diagonal_of(square):
    rows, columns = iotas(square.shape)
    return jnp.sum(jnp.where(rows == columns, square, 0.0), axis=0, keepdims=True)


def pack(square):
    half = square.shape[0] // 2
    rows, columns = iotas((half, 2 * half))
    lower = jnp.concatenate([square[half:, half:], square[half:, :half]], axis=1)
    return jnp.where(columns >= rows, square[:half], lower)


def unpack(packed, diagonal):
    half = packed.shape[0]
    rows, columns = iotas(packed.shape)
    top = jnp.where(columns > rows, packed, 0.0)
    turned = jnp.concatenate([packed[:, half:], packed[:, :half]], axis=1)
    keep = jnp.logical_and(columns >= half, columns - half < rows)
    strict = jnp.concatenate([top, jnp.where(keep, turned, 0.0)], axis=0)
    rows, columns = iotas(strict.shape)
    return strict + strict.T + jnp.where(rows == columns, diagonal, 0.0)


def row_of(user, n_tp):
    rank = user % n_tp
    return rank if n_tp % 2 else rank // 2 + rank % 2 * (n_tp // 2)


def user_of(place, group, per_row, n_tp):
    row, c = place // group, place % group
    rank = row if n_tp % 2 else row % (n_tp // 2) * 2 + row // (n_tp // 2)
    return c % per_row * n_tp + rank, c // per_row


def place_of(user, slot, group, per_row, n_tp):
    return row_of(user, n_tp) * group + slot * per_row + user // n_tp


def first_kernel(wanted, pieces, codes_ref, g_ref, m_ref, *refs):
    count = len(wanted)
    outs = refs[:count]
    g_buf, m_buf, g_sem, m_sem = refs[count:]
    rows = g_buf.shape[2]
    group = codes_ref.shape[1] // lax.axis_size("tp")
    row = lax.axis_index("tp")

    def in_copies(i, p, source):
        part = pl.ds(p * rows, rows)
        return (
            pltpu.make_async_copy(g_ref.at[source, part], g_buf.at[i, p], g_sem.at[i, p]),
            pltpu.make_async_copy(m_ref.at[source, part], m_buf.at[i, p], m_sem.at[i, p]),
        )

    reads = []
    for i, (partner, c) in enumerate(wanted):
        place = partner(row) * group + c
        source = jnp.int32(0)
        for j in range(codes_ref.shape[1]):
            source = jnp.where(codes_ref[0, j] == place, j, source)
        for p in range(pieces):
            reads.append((i, p, in_copies(i, p, source)))
            for copy in reads[-1][2]:
                copy.start()
    for i, p, copies in reads:
        for copy in copies:
            copy.wait()
        _, y = nesterov_of(g_buf[i, p], m_buf[i, p])
        outs[i][0, p * rows : (p + 1) * rows] = y


def first_blocks(codes, grads, momentum, wanted, pieces=4):
    _, head, width = grads.shape
    count = len(wanted)
    buffer = pltpu.VMEM((count, pieces, head // pieces, width), jnp.bfloat16)
    return pl.pallas_call(
        functools.partial(first_kernel, wanted, pieces),
        out_shape=[pltpu.VMEM((1, head, width), jnp.bfloat16)] * count,
        in_specs=[SMEM, HBM, HBM],
        out_specs=[VMEM] * count,
        scratch_shapes=[buffer] * 2 + [pltpu.SemaphoreType.DMA((count, pieces))] * 2,
        compiler_params=params_beside(grads),
    )(codes, grads, momentum)


def all_kernel(spans, spread, tile, source, place, g_ref, m_ref, newm_ref, parts_ref, *refs):
    outs = refs[: len(spans)]
    g_buf, m_buf, v_buf, y_buf, g_sem, m_sem, v_sem, y_sem = refs[len(spans) :]
    blocks, head, width = g_buf.shape
    half = head // 2
    users = blocks // spread
    n_tp = lax.axis_size("tp")
    per_row = users // n_tp

    def in_copies(i):
        return (
            pltpu.make_async_copy(g_ref.at[source[i]], g_buf.at[i], g_sem.at[i]),
            pltpu.make_async_copy(m_ref.at[source[i]], m_buf.at[i], m_sem.at[i]),
        )

    def newm_copy(i):
        return pltpu.make_async_copy(v_buf.at[i], newm_ref.at[source[i]], v_sem.at[i])

    @pl.loop(0, blocks)
    def _(i):
        for copy in in_copies(i):
            copy.start()

    for f in range(users, parts_ref.shape[0]):
        parts_ref[f, : spread * half] = jnp.zeros((spread * half, head), jnp.float32)

    @pl.loop(0, blocks)
    def _(i):
        for copy in in_copies(i):
            copy.wait()
        gram = jnp.zeros((head, head), jnp.float32)
        for k in range(0, width, tile):
            part = pl.ds(k, tile)
            velocity, y = nesterov_of(g_buf[i, :, part], m_buf[i, :, part])
            v_buf[i, :, part] = velocity.astype(jnp.bfloat16)
            y_buf[i, :, part] = y
            gram = gram + lax.dot_general(
                y, y, (((1,), (1,)), ((), ())), preferred_element_type=jnp.float32
            )
        newm_copy(i).start()
        for (start, count), out in zip(spans, outs):

            @pl.when(jnp.logical_and(i >= start, i < start + count))
            def _():
                pltpu.make_async_copy(y_buf.at[i], out.at[i - start], y_sem.at[i]).start()

        to, slot = user_of(place[i], blocks // n_tp, per_row, n_tp)
        at = pl.multiple_of(slot * half, half)
        parts_ref[to, pl.ds(at, half)] = pack(gram)
        diagonal = diagonal_of(gram)
        for f in range(parts_ref.shape[0]):
            parts_ref[f, pl.ds(spread * half + place[i], 1)] = diagonal

    @pl.loop(0, blocks)
    def _(i):
        newm_copy(i).wait()

    for (start, count), out in zip(spans, outs):
        for k in range(count):
            i = start + k
            pltpu.make_async_copy(y_buf.at[i], out.at[k], y_sem.at[i]).wait()


def all_blocks(source, place, grads, momentum, spans, spread, devices):
    blocks, head, width = grads.shape
    buffer = pltpu.VMEM(grads.shape, jnp.bfloat16)
    return pl.pallas_call(
        functools.partial(all_kernel, spans, spread, min(width, 256)),
        out_shape=[
            jax.ShapeDtypeStruct(grads.shape, jnp.bfloat16),
            jax.ShapeDtypeStruct((devices, spread * head // 2 + blocks, head), jnp.float32),
        ]
        + [jax.ShapeDtypeStruct((count, head, width), jnp.bfloat16) for _, count in spans],
        in_specs=[SMEM, SMEM, HBM, HBM],
        out_specs=[HBM, VMEM] + [HBM] * len(spans),
        scratch_shapes=[buffer] * 4 + [pltpu.SemaphoreType.DMA((blocks,))] * 4,
        compiler_params=params_beside(grads),
        name="all_blocks",
    )(source, place, grads, momentum)


def iterate(work):
    def dot(a, b):
        return jnp.dot(a, b, precision=lax.Precision.HIGHEST, preferred_element_type=jnp.float32)

    head = work[0][0].shape[1]
    rows, columns = iotas((head, head))
    identity = jnp.where(rows == columns, 1.0, 0.0)
    inverses = [1.0 / (jnp.sqrt(jnp.sum(d, axis=1, keepdims=True)) + epsilon) for _, d in work]
    grams = [unpack(p, d) * (inv * inv) for (p, d), inv in zip(work, inverses)]
    turned = [None] * len(work)
    for i in range(ITERS):
        last = i + 1 == ITERS
        squared = [dot(g, g) for g in grams]
        mixed = [poly_linear * identity + poly_cubic * g + poly_quintic * s for g, s in zip(grams, squared)]
        right = [None if last else dot(g, m) for g, m in zip(grams, mixed)]
        turned = [m if q is None else dot(m, q) for q, m in zip(turned, mixed)]
        grams = [None if last else dot(m, r) for m, r in zip(mixed, right)]
    turned = [q * inv for q, inv in zip(turned, inverses)]
    return [(pack(q), diagonal_of(q)) for q in turned]


def write_packed(ref, solved):
    head = ref.shape[1]
    half, count = head // 2, len(solved)
    for k, (packed, diagonal) in enumerate(solved):
        ref[k * half : (k + 1) * half] = packed
        ref[count * half + k : count * half + k + 1] = diagonal
    used = count * half + count
    ref[used:] = jnp.zeros((ref.shape[0] - used, head), jnp.float32)


def packed_rows(count, head):
    return count * head // 2 + 8 * -(-count // 8)


def solve_kernel(spread, skip, count, elements, owners, codes, parts_ref, *refs):
    slot_ref, sum_ref = refs[-2:]
    n_fsdp, _, head = parts_ref.shape
    half = head // 2
    here = lax.axis_index("fsdp")
    n_tp = lax.axis_size("tp")
    per_row = count // spread // n_tp
    total = parts_ref[0]
    for f in range(1, n_fsdp):
        total = total + parts_ref[f]
    diagonals = total[spread * half :]
    squares = jnp.sum(diagonals, axis=1, keepdims=True)
    sum_ref[:count] = diagonals
    sum_ref[count:] = jnp.broadcast_to(jnp.sqrt(squares / elements), (count, head))
    _, lanes = iotas((1, head))
    slots = jnp.zeros((1, head), jnp.float32)
    taken = jnp.int32(0)
    for j in range(count):
        mine = owners[j, 0] == here
        value = sum_ref[pl.ds(count + codes[0, j], 1)]
        slots = slots + jnp.where(jnp.logical_and(mine, lanes == taken), value, 0.0)
        taken = taken + mine.astype(jnp.int32)
    slot_ref[...] = slots

    work = []
    for k in range(spread):
        at = jnp.minimum(place_of(here, k, spread * per_row, per_row, n_tp), count - 1)
        work.append((total[k * half : (k + 1) * half], sum_ref[pl.ds(at, 1)]))
    solved = iterate(work)
    write_packed(refs[0], solved)
    if skip:
        write_packed(refs[1], solved[skip:])


def solve(parts, owners, codes, spread, skip, elements):
    _, _, head = parts.shape
    count = codes.shape[1]
    outs = [packed_rows(spread, head)] + ([packed_rows(spread - skip, head)] if skip else [])
    return pl.pallas_call(
        functools.partial(solve_kernel, spread, skip, count, elements),
        out_shape=[jax.ShapeDtypeStruct((n, head), jnp.float32) for n in outs + [1]],
        in_specs=[SMEM, SMEM, VMEM],
        out_specs=[VMEM] * (len(outs) + 1),
        scratch_shapes=[pltpu.VMEM((2 * count, head), jnp.float32)],
        compiler_params=params(4 * parts.size * 4),
        name="solve",
    )(owners, codes, parts)


def far_kernel(members, per_row, *refs):
    parts_ref = refs[-1]
    head = parts_ref.shape[2]
    half = head // 2
    row = lax.axis_index("tp")
    parts_ref[...] = jnp.zeros(parts_ref.shape, jnp.float32)
    for (source_row, c), ref in zip(members, refs):
        y = ref[0]
        gram = lax.dot_general(y, y, (((1,), (1,)), ((), ())), preferred_element_type=jnp.float32)
        to = source_row(row) * per_row + c
        parts_ref[to, :half] = pack(gram)
        parts_ref[to, half : half + 1] = diagonal_of(gram)


def far_parts(arrays, members, per_row, devices):
    head = arrays[0].shape[1]
    return pl.pallas_call(
        functools.partial(far_kernel, members, per_row),
        out_shape=pltpu.VMEM((devices, packed_rows(1, head), head), jnp.float32),
        in_specs=[VMEM] * len(arrays),
        out_specs=VMEM,
        compiler_params=params(8 * devices * packed_rows(1, head) * head * 4),
        name="far_parts",
    )(*arrays)


def finish_kernel(spread, per_row, parts_ref, same_ref, cross_ref, out_ref):
    n_fsdp, _, head = parts_ref.shape
    half = head // 2
    middle = lax.axis_size("tp") // 2
    source_row = lax.axis_index("fsdp") // per_row
    crossed = (source_row >= middle) != (lax.axis_index("tp") >= middle)
    total = parts_ref[0]
    for f in range(1, n_fsdp):
        total = total + parts_ref[f]
    solved = iterate([(total[:half], total[half : half + 1])])
    sent = spread - 1
    for k in range(sent):
        diagonal = cross_ref[sent * half + k : sent * half + k + 1]
        solved.append((cross_ref[k * half : (k + 1) * half], diagonal))
    chosen = []
    for k, (packed, diagonal) in enumerate(solved):
        other = same_ref[k * half : (k + 1) * half]
        other_diagonal = same_ref[spread * half + k : spread * half + k + 1]
        chosen.append((jnp.where(crossed, packed, other), jnp.where(crossed, diagonal, other_diagonal)))
    write_packed(out_ref, chosen)


def finish(parts, same, cross, spread, per_row):
    return pl.pallas_call(
        functools.partial(finish_kernel, spread, per_row),
        out_shape=jax.ShapeDtypeStruct(same.shape, jnp.float32),
        in_specs=[VMEM] * 3,
        out_specs=VMEM,
        compiler_params=params(8 * parts.size * 4),
        name="finish",
    )(parts, same, cross)


def unpack_kernel(spread, per_row, packed_ref, out_ref):
    head = packed_ref.shape[2]
    half = head // 2

    @pl.loop(0, out_ref.shape[0] // spread)
    def _(f):
        for k in range(spread):
            packed = packed_ref[f, k * half : (k + 1) * half]
            q = unpack(packed, packed_ref[f, spread * half + k : spread * half + k + 1])
            high = q.astype(jnp.bfloat16)
            place = (f // per_row * spread + k) * per_row + f % per_row
            out_ref[place, :, :head] = high
            out_ref[place, :, head:] = (q - high.astype(jnp.float32)).astype(jnp.bfloat16)


def unpack_all(packed, spread, per_row, blocks):
    head = packed.shape[2]
    return pl.pallas_call(
        functools.partial(unpack_kernel, spread, per_row),
        out_shape=jax.ShapeDtypeStruct((blocks, head, 2 * head), jnp.bfloat16),
        in_specs=[VMEM],
        out_specs=VMEM,
        compiler_params=params(4 * packed.size * 4),
        name="unpack_all",
    )(packed)


def apply_kernel(factor, members, at_end, tiles, q_ref, *refs):
    out = refs[-3]
    u_buf, u_sem = refs[-2:]
    width = u_buf.shape[2] // tiles
    row = lax.axis_index("tp")

    def u_copy(i, j):
        part = pl.ds(j * width, width)
        return pltpu.make_async_copy(u_buf.at[i, :, part], out.at[places[i], :, part], u_sem.at[i, j])

    places = [place_at(row) for place_at, _, _ in members]

    def update(i, way, k):
        q = q_ref[places[i]]
        for j in range(tiles):
            part = pl.ds(j * width, width)
            y = refs[way][k, :, part]
            y = jnp.concatenate([y, y], axis=0)
            ortho = jnp.dot(q, y, preferred_element_type=jnp.float32)
            ortho = ortho.astype(jnp.bfloat16).astype(jnp.float32)
            u_buf[i, :, part] = (-factor * ortho).astype(jnp.bfloat16)
            u_copy(i, j).start()

    if len(members[0][1]) == 1:
        for i, (_, ways, k) in enumerate(members):
            update(i, ways[0], k)
    else:
        for way, here in ((0, at_end(row)), (1, jnp.logical_not(at_end(row)))):

            @pl.when(here)
            def _():
                for i, (_, ways, k) in enumerate(members):
                    update(i, ways[way], k)

    for i in range(len(members)):
        for j in range(tiles):
            u_copy(i, j).wait()


def apply_blocks(factor, transforms, chunks, into, at_end, tiles):
    arrays, members = [], []
    for ways, places in chunks:
        at = range(len(arrays), len(arrays) + len(ways))
        arrays += ways
        members += [(place_at, at, k) for k, place_at in enumerate(places)]
    head, width = arrays[0].shape[1:]
    blocks = transforms.shape[0]
    total = len(members)
    in_specs = [VMEM] * (1 + len(arrays))
    operands = [transforms, *arrays]
    aliases = {}
    if into is not None:
        aliases = {len(operands): 0}
        in_specs.append(HBM)
        operands.append(into)
    return pl.pallas_call(
        functools.partial(apply_kernel, factor, members, at_end, tiles),
        out_shape=jax.ShapeDtypeStruct((blocks, head, width), jnp.bfloat16),
        in_specs=in_specs,
        out_specs=HBM,
        scratch_shapes=[
            pltpu.VMEM((total, head, width), jnp.bfloat16),
            pltpu.SemaphoreType.DMA((total, tiles)),
        ],
        input_output_aliases=aliases,
        compiler_params=params(4 * total * head * width * 2),
        name="apply_blocks",
    )(*operands)


def local(grads, momentum, owner_table, pool_map):
    n_fsdp, n_tp = lax.axis_size("fsdp"), lax.axis_size("tp")
    row = lax.axis_index("tp")
    blocks, head, width = grads.shape
    group = blocks // n_tp
    spread = -(-blocks // n_fsdp)
    paired = n_tp & (n_tp - 1) == 0

    def partner(t, x):
        return t ^ x if paired else (t + x) % n_tp

    def sender(t, x):
        return t ^ x if paired else (t - x) % n_tp

    far = [x for x in reversed(range(1, n_tp)) if x >= n_tp // 2]
    near = [x for x in range(1, n_tp) if x < n_tp // 2]
    cut = max(1, group // 2)

    def singles(partners, places):
        return [(x, (c,)) for c in places for x in partners]

    first = singles(far, range(1))
    early = first + singles(far, range(1, cut)) + singles(near, range(cut - 1))
    late = singles(near, range(cut - 1, cut))
    for c in range(cut, group - 1):
        late += singles(far, [c]) + singles(near, [c])
    late += singles(near, [group - 1]) if group > cut else []
    last = singles(far, range(max(cut, group - 1), group))
    late += last
    own = [(0, tuple(range(group)))]
    chunks = early + late + own
    steps = [(x, c) for x, cs in chunks for c in cs]

    codes = pool_map[0]
    position = jnp.arange(blocks, dtype=jnp.int32)
    offsets = jnp.array([c for _, c in steps], jnp.int32)
    partners = jnp.array([x for x, _ in steps], jnp.int32)
    place_out = partner(row, partners) * group + offsets
    source = jnp.sum(jnp.where(codes[None, :] == place_out[:, None], position[None, :], 0), axis=1)

    starts, total = {}, 0
    for chunk in chunks:
        starts[chunk] = (total, len(chunk[1]))
        total += len(chunk[1])

    def at_end(t):
        return jnp.logical_or(t < n_tp // 4, t >= n_tp - n_tp // 4)

    ends = [t for t in range(n_tp) if t < n_tp // 4 or t >= n_tp - n_tp // 4]
    sends = [(chunk, None) for chunk in early + late if chunk not in last]
    if ends:
        sends += [(chunk, side) for side in (0, 1) for chunk in last]
    else:
        sends += [(chunk, None) for chunk in last]
    got = {}

    def send(chunk, side, array):
        pairs = [(t, partner(t, chunk[0])) for t in range(n_tp)]
        if side is not None:
            pairs = [(t, to) for t, to in pairs if (to in ends) == (side == 0)]
        got[chunk, side] = lax.ppermute(array, "tp", pairs)

    for some in (first[:1], first[1:]):
        wanted = [(functools.partial(partner, x=x), cs[0]) for x, cs in some]
        arrays = first_blocks(pool_map, grads, momentum, wanted) if some else []
        for chunk, array in zip(some, arrays):
            send(chunk, None, array)
    rest = chunks[len(first) :]
    new_momentum, parts, *ys = all_blocks(
        source, place_out, grads, momentum, [starts[chunk] for chunk in rest], spread, n_fsdp
    )
    ys = dict(zip(rest, ys))
    for chunk, side in sends[len(first) :]:
        send(chunk, side, ys[chunk])

    parts = lax.all_to_all(parts, "fsdp", split_axis=0, concat_axis=0, tiled=True)
    per_row = group // spread
    skip = 1 if paired and spread > 1 else 0
    *packed, slots = solve(parts, owner_table, pool_map, spread, skip, head * width * n_fsdp)
    same_pairs, cross_pairs = [], []
    for f in range(blocks // spread):
        for t in range(n_tp):
            row_to = row_of(f, n_tp)
            pair = (f * n_tp + t, (t * per_row + f // n_tp) * n_tp + row_to)
            crosses = skip and (t < n_tp // 2) != (row_to < n_tp // 2)
            (cross_pairs if crosses else same_pairs).append(pair)
    if skip:
        cross = lax.ppermute(packed[1], ("fsdp", "tp"), cross_pairs)
    packed = lax.ppermute(packed[0], ("fsdp", "tp"), same_pairs)
    if skip:
        arrived = singles(far, range(per_row))
        members = [(functools.partial(sender, x=x), cs[0]) for x, cs in arrived]
        parts = far_parts([got[chunk, None] for chunk in arrived], members, per_row, n_fsdp)
        parts, packed, cross = lax.optimization_barrier((parts, packed, cross))
        parts = lax.all_to_all(parts, "fsdp", split_axis=0, concat_axis=0, tiled=True)
        packed = finish(parts, packed, cross, spread, per_row)
    packed = jnp.broadcast_to(packed[None], (n_fsdp,) + packed.shape)
    packed = lax.all_to_all(packed, "fsdp", split_axis=0, concat_axis=0, tiled=True)
    transforms = unpack_all(packed, spread, per_row, blocks)

    factor = step_size * 0.2 * math.sqrt(width * n_fsdp)
    for chunk in own:
        got[chunk, None] = ys[chunk]

    def arrival(chunk):
        x, cs = chunk
        ways = [got[chunk, side] for side in (0, 1, None) if (chunk, side) in got]
        return ways, [functools.partial(lambda t, c: sender(t, x) * group + c, c=c) for c in cs]

    update = None
    between = [chunk for chunk in late if chunk not in last]
    for members in [own + early] + ([between] if between else []) + [last]:
        tiles = 1 if len(members) > 2 or width < 512 else 4
        update = apply_blocks(factor, transforms, [arrival(m) for m in members], update, at_end, tiles)
    return (new_momentum, update, slots[:, :CAP])


def solution(mesh):
    def step(*args):
        return local(*args)

    in_specs = (P("tp", None, "fsdp"), P("tp", None, "fsdp"), P("tp", None), P("tp", None))
    out_specs = (P("tp", None, "fsdp"), P("tp", None, "fsdp"), P("tp", "fsdp"))
    step = jax.shard_map(step, mesh=mesh, in_specs=in_specs, out_specs=out_specs, check_vma=False)
    return step
```
